128 devices in a mesh: grp: 4 (over y_lo, core), gx: 32 (over y_hi, z, x).
Axes of the slice: x: 4, y: 4 (y_hi: 2, y_lo: 2; y = y_hi * 2 + y_lo), z: 4, core: 2. Of those that a mesh axis runs over, the one named last changes fastest.
Arguments:
- ocean_fields: float32 [4, 128, 32768], P(None, 'grp', 'gx'), may hold values from -1 to 1
- tracers: float32 [19, 128, 32768], P(None, ('grp', 'gx')), may hold values from 0.1 to 4
- wet_levels: int32 [128, 512], P(('grp', 'gx')), may hold values from 0 to 64
- interaction: float32 [19, 19], replicated, may hold values from -1.25 to 1.25
Outputs:
- ocean_next: float32 [4, 128, 32768], P(None, 'grp', 'gx')
- tracers_next: float32 [19, 128, 32768], P(None, ('grp', 'gx'))
The draws below stay inside these ranges and needn't reach their ends.
All inputs are finite; a program needn't handle non-finite values.
Results may differ from the reference program's by a relative error of at most 0.0001.
Values sent between devices are 32-bit elements; how exact they have to be, the bound alone decides.
No kernel may reach another device: no remote copies, remote signals or barrier semaphores. Data moves between devices by JAX's collectives and lax.ppermute only.
A program may use at most 128 MiB of HBM per device.

```python
import math
import jax
import jax.numpy as jnp
from jax import lax

L = 64
NTR = 19
NC = 2
NB = 2
NY = 128
NX = 512


def with_ends(array, key, least, top_value):
    spot = [jax.random.randint(jax.random.fold_in(key, axis), (), 0, length) for axis, length in enumerate(array.shape)]
    widest = array.shape.index(max(array.shape))
    neighbour = spot[:widest] + [(spot[widest] + 1) % array.shape[widest]] + spot[widest + 1:]
    return array.at[tuple(spot)].set(least).at[tuple(neighbour)].set(top_value)


def steps_of(own_key, shape, cuts, low, top_value):
    gain, own = 1.0, jax.random.fold_in(own_key, 6)
    for dim, blocks in cuts:
        draws = jnp.exp(jax.random.uniform(jax.random.fold_in(own, dim), (blocks,), jnp.float32, low / len(cuts), top_value / len(cuts)))
        gain = gain * jnp.repeat(draws, shape[dim] // blocks).reshape([-1 if axis == dim else 1 for axis in range(len(shape))])
    return gain


def centred(key, dims, scale, reach, held_as=jnp.bfloat16):
    array = jax.random.normal(key, dims, jnp.float32) * scale
    return jnp.minimum(jnp.maximum(array, -reach), reach).astype(held_as)


def setup_inputs(seed: int = 0) -> dict:
    seeds = jax.random.split(jax.random.key(seed), 5)
    return {
        "ocean_fields": jnp.clip(jax.random.uniform(seeds[0], (4, NY, NX * L), jnp.float32, -1.0, 1.0) * steps_of(seeds[0], (4, NY, NX * L), ((1, 4), (2, 32)), -0.4, 0.0), -1.0, 1.0),
        "tracers": jnp.clip(jnp.exp(math.log(4.0) - 3.6888794 * jax.random.uniform(seeds[1], (NTR, NY, NX * L), jnp.float32) ** steps_of(seeds[1], (NTR, NY, NX * L), ((1, 128),), -0.2, 0.2)), 0.1, 4.0),
        "wet_levels": with_ends(jax.random.randint(seeds[2], (NY, NX), 0, L + 1), jax.random.fold_in(seeds[2], 1), 0, L).astype(jnp.int32),
        "interaction": centred(seeds[3], (NTR, NTR), NTR ** -0.5, 1.25, jnp.float32),
    }


courant = 0.2
diffusion = 0.08
viscosity = 0.08
time_step = 0.1
thermal = 0.2
haline = 0.15
gravity = 0.1
coriolis = 0.5
coriolis_slope = 0.5
water_extinction = 0.04
pigment_extinction = 0.01
heating_rate = 0.5
light_half = 0.3
warming = 0.1
saturation = 0.5
reaction = 0.5


def neighbours(padded):
    centre = padded[..., 1:-1, 1:-1, :]
    cell_east = padded[..., 1:-1, 2:, :]
    cell_west = padded[..., 1:-1, :-2, :]
    cell_north = padded[..., 2:, 1:-1, :]
    cell_south = padded[..., :-2, 1:-1, :]
    return centre, cell_east, cell_west, cell_north, cell_south


def upper_ones(levels):
    level_ids = jnp.arange(levels)
    return (level_ids[:, None] <= level_ids[None, :]).astype(jnp.float32)


def light_profile(pigment, triangle):
    extinct = water_extinction + pigment_extinction * pigment
    optical = jnp.matmul(extinct, triangle, precision=lax.Precision.HIGHEST) - 0.5 * extinct
    return extinct, jnp.exp(-optical)


def wet_levels_mask(depth_cells, levels):
    level_ids = jnp.arange(levels).astype(jnp.float32)
    return (level_ids < depth_cells[..., None]).astype(jnp.float32)


def upwind_change(cells, face_tuple):
    centre, cell_east, cell_west, cell_north, cell_south = cells
    face_east, face_west, face_north, face_south = face_tuple
    flux_east = jnp.maximum(face_east, 0.0) * centre + jnp.minimum(face_east, 0.0) * cell_east
    flux_west = jnp.maximum(face_west, 0.0) * cell_west + jnp.minimum(face_west, 0.0) * centre
    flux_north = jnp.maximum(face_north, 0.0) * centre + jnp.minimum(face_north, 0.0) * cell_north
    flux_south = jnp.maximum(face_south, 0.0) * cell_south + jnp.minimum(face_south, 0.0) * centre
    return courant * (flux_east - flux_west + flux_north - flux_south)


def laplacian(cells, open_faces):
    summed = open_faces[0] * (cells[1] - cells[0]) + open_faces[1] * (cells[2] - cells[0])
    return summed + open_faces[2] * (cells[3] - cells[0]) + open_faces[3] * (cells[4] - cells[0])


def ocean_update(fields_pad, depth_pad, pigment, row_index, total_rows):
    levels = fields_pad.shape[-1]
    triangle = upper_ones(levels)
    wet_pad = wet_levels_mask(depth_pad, levels)
    wet_parts = neighbours(wet_pad)
    wet_mask = wet_parts[0]
    open_faces = (wet_mask * wet_parts[1], wet_mask * wet_parts[2], wet_mask * wet_parts[3], wet_mask * wet_parts[4])
    density = (haline * fields_pad[3] - thermal * fields_pad[2]) * wet_pad
    pressure = gravity * jnp.matmul(density, triangle, precision=lax.Precision.HIGHEST)
    pressure_parts = neighbours(pressure)
    zonal_parts = neighbours(fields_pad[0])
    meridional = neighbours(fields_pad[1])
    warmth = neighbours(fields_pad[2])
    salt_parts = neighbours(fields_pad[3])
    face_east = 0.5 * (zonal_parts[0] + zonal_parts[1]) * open_faces[0]
    face_west = 0.5 * (zonal_parts[0] + zonal_parts[2]) * open_faces[1]
    face_north = 0.5 * (meridional[0] + meridional[3]) * open_faces[2]
    face_south = 0.5 * (meridional[0] + meridional[4]) * open_faces[3]
    face_tuple = (face_east, face_west, face_north, face_south)
    slope_x = 0.5 * (open_faces[0] * (pressure_parts[1] - pressure_parts[0]) + open_faces[1] * (pressure_parts[0] - pressure_parts[2]))
    slope_y = 0.5 * (open_faces[2] * (pressure_parts[3] - pressure_parts[0]) + open_faces[3] * (pressure_parts[0] - pressure_parts[4]))
    latitude = (row_index + 0.5) / total_rows - 0.5
    coriolis_row = (coriolis + coriolis_slope * latitude)[:, None, None]
    extinct, irradiance = light_profile(pigment, triangle)
    heating = heating_rate * extinct * irradiance
    zonal_next = (zonal_parts[0] + time_step * (coriolis_row * meridional[0] - slope_x) + viscosity * laplacian(zonal_parts, open_faces)) * wet_mask
    merid_next = (meridional[0] + time_step * (-coriolis_row * zonal_parts[0] - slope_y) + viscosity * laplacian(meridional, open_faces)) * wet_mask
    warm_next = (warmth[0] - upwind_change(warmth, face_tuple) + diffusion * laplacian(warmth, open_faces) + heating) * wet_mask
    salt_next = (salt_parts[0] - upwind_change(salt_parts, face_tuple) + diffusion * laplacian(salt_parts, open_faces)) * wet_mask
    return jnp.stack([zonal_next, merid_next, warm_next, salt_next]), face_tuple


def react_tracers(advected, warmth, depth_cells, interaction):
    levels = advected.shape[-1]
    irradiance = light_profile(advected[0], upper_ones(levels))[1]
    wet_mask = wet_levels_mask(depth_cells, levels)
    growth = irradiance / (irradiance + light_half) * jnp.exp(warming * warmth) * wet_mask
    saturated = advected / (saturation + jnp.abs(advected))
    mixing = jnp.dot(interaction, saturated.reshape(saturated.shape[0], -1), precision=lax.Precision.HIGHEST)
    return advected + reaction * growth * mixing.reshape(advected.shape)


def advect_all(stocks, face_tuple):
    def advect_one(tracer_field):
        padded = jnp.pad(tracer_field, ((1, 1), (1, 1), (0, 0)))
        cells = neighbours(padded)
        return cells[0] - upwind_change(cells, face_tuple)
    return lax.map(advect_one, stocks)


def reference(ocean_fields, tracers, wet_levels, interaction):
    total_rows = ocean_fields.shape[1]
    columns = wet_levels.shape[1]
    fields = ocean_fields.reshape(4, total_rows, columns, L)
    stocks = tracers.reshape(NTR, total_rows, columns, L)
    depth_cells = wet_levels.astype(jnp.float32)
    depth_pad = jnp.pad(depth_cells, 1)
    row_index = jnp.arange(total_rows).astype(jnp.float32)
    for coupling in range(NC):
        fields_pad = jnp.pad(fields, ((0, 0), (1, 1), (1, 1), (0, 0)))
        fields, face_tuple = ocean_update(fields_pad, depth_pad, stocks[0], row_index, total_rows)
        for substep in range(NB):
            stocks = react_tracers(advect_all(stocks, face_tuple), fields[2], depth_cells, interaction)
    return fields.reshape(4, total_rows, columns * L), stocks.reshape(NTR, total_rows, columns * L)
```

```python
import jax
import jax.numpy as jnp
from jax import lax
from jax.experimental import pallas as pl
from jax.experimental.pallas import tpu as pltpu
from jax.sharding import PartitionSpec as P

NC = 2
NB = 2
HALO = NC * NB

courant = 0.2
diffusion = 0.08
viscosity = 0.08
time_step = 0.1
thermal = 0.2
haline = 0.15
gravity = 0.1
coriolis = 0.5
coriolis_slope = 0.5
water_extinction = 0.04
pigment_extinction = 0.01
heating_rate = 0.5
light_half = 0.3
warming = 0.1
saturation = 0.5
reaction = 0.5

LANES = 128
ROWS8 = 8
F32 = jnp.float32
BF16 = jnp.bfloat16


def window_kernel(strip, depth_plane, out, big, sem_in, sem_out):
    planes, lines = big.shape[0], strip.shape[1]
    tiles, wide = out.shape[0], out.shape[2]
    step = lines // tiles
    edge = (wide - step) // 2
    tracers_in = pltpu.make_async_copy(strip, big.at[pl.ds(0, planes - 1), pl.ds(edge, lines)], sem_in.at[0])
    depth_in = pltpu.make_async_copy(depth_plane, big.at[pl.ds(planes - 1, 1), pl.ds(edge, lines)], sem_in.at[1])
    tracers_in.start()
    depth_in.start()
    zeros = jnp.zeros((planes, edge, 1, LANES), F32)
    big[:, pl.ds(0, edge)] = zeros
    big[:, pl.ds(edge + lines, edge)] = zeros
    tracers_in.wait()
    depth_in.wait()

    def send(d):
        return pltpu.make_async_copy(big.at[:, pl.ds(d * step, wide)], out.at[d], sem_out.at[d])

    @pl.loop(0, tiles)
    def _(d):
        send(d).start()

    @pl.loop(0, tiles)
    def _(d):
        send(d).wait()


def cut_windows(strip, depth_plane, tiles, wide):
    planes = strip.shape[0] + 1
    lines = strip.shape[1]
    edge = (wide - lines // tiles) // 2
    anywhere = pl.BlockSpec(memory_space=pl.ANY)
    return pl.pallas_call(
        window_kernel,
        out_shape=jax.ShapeDtypeStruct((tiles, planes, wide, 1, LANES), F32),
        in_specs=[anywhere, anywhere],
        out_specs=anywhere,
        scratch_shapes=[
            pltpu.VMEM((planes, lines + 2 * edge, 1, LANES), F32),
            pltpu.SemaphoreType.DMA((2,)),
            pltpu.SemaphoreType.DMA((tiles,)),
        ],
        name="cut_windows",
    )(strip, depth_plane)


def main_kernel(
    tile, south, north, ocean, ocean_south, ocean_north, mix_ref, ocean_out, out,
    raw, stock_a, stock_b, sea, ocean_a, ocean_b, press, wet, weights, growth0, result, sem,
):
    ntr = stock_a.shape[2]
    ncp, nrt = stock_a.shape[0], stock_a.shape[1]
    planes = ntr + 1
    line_stride = planes * ncp
    rows = tile.shape[0] // line_stride
    halo = HALO
    inner = ncp - halo
    copies = [
        pltpu.make_async_copy(south, raw.at[pl.ds(0, halo * line_stride)], sem.at[0]),
        pltpu.make_async_copy(tile, raw.at[pl.ds(halo * line_stride, rows * line_stride)], sem.at[1]),
        pltpu.make_async_copy(north, raw.at[pl.ds((halo + rows) * line_stride, halo * line_stride)], sem.at[2]),
    ]
    for copy in copies:
        copy.start()

    lane = lax.broadcasted_iota(jnp.int32, (ROWS8, LANES), 1)
    sub = lax.broadcasted_iota(jnp.int32, (ROWS8, LANES), 0)
    half = LANES // 2
    level = lane % half
    left = lane < half
    level_f = level.astype(F32)

    def roll_lanes(x, by):
        return pltpu.roll(x, by, x.ndim - 1)

    def roll_rows(x, by):
        return pltpu.roll(x, by, x.ndim - 2)

    def running_sum(x):
        by = 1
        while by < half:
            x = x + jnp.where(level >= by, roll_lanes(x, by), 0.0)
            by *= 2
        return x

    def around(ref, cp, rt, *more):
        up = ref[(cp, jnp.minimum(rt + 1, nrt - 1), *more)]
        down = ref[(cp, jnp.maximum(rt - 1, 0), *more)]
        right = ref[(jnp.minimum(cp + 1, ncp - 1), rt, *more)]
        leftward = ref[(jnp.maximum(cp - 1, 0), rt, *more)]
        centre = ref[(cp, rt, *more)]
        cell_north = roll_rows(jnp.where(sub == 0, up, centre), ROWS8 - 1)
        cell_south = roll_rows(jnp.where(sub == ROWS8 - 1, down, centre), 1)
        swapped = roll_lanes(centre, half)
        far = roll_lanes(jnp.where(left, right, leftward), half)
        return centre, swapped, far, cell_north, cell_south

    def five(ref, cp, rt, *more):
        centre, swapped, far, cell_north, cell_south = around(ref, cp, rt, *more)
        return centre, jnp.where(left, swapped, far), jnp.where(left, far, swapped), cell_north, cell_south

    for f in range(4):
        sea[f, pl.ds(0, halo), :] = ocean_south[f]
        sea[f, pl.ds(halo, rows), :] = ocean[f]
        sea[f, pl.ds(halo + rows, halo), :] = ocean_north[f]
    for cp in range(ncp):
        for f in range(4):
            for rt in range(nrt):
                ocean_a[cp, rt, f] = sea[f, pl.ds(rt * ROWS8, ROWS8), pl.ds(cp * LANES, LANES)]

    wide = ntr * ROWS8
    pick = (lax.broadcasted_iota(jnp.int32, (wide, ntr), 0) // ROWS8 == lax.broadcasted_iota(jnp.int32, (wide, ntr), 1)).astype(F32)
    pick_t = (lax.broadcasted_iota(jnp.int32, (ntr, wide), 1) // ROWS8 == lax.broadcasted_iota(jnp.int32, (ntr, wide), 0)).astype(F32)
    spread = jnp.dot(
        jnp.dot(pick, mix_ref[...], precision=lax.Precision.HIGHEST, preferred_element_type=F32),
        pick_t, precision=lax.Precision.HIGHEST, preferred_element_type=F32,
    )
    same = lax.broadcasted_iota(jnp.int32, (wide, wide), 0) % ROWS8 == lax.broadcasted_iota(jnp.int32, (wide, wide), 1) % ROWS8
    spread = jnp.where(same, spread, 0.0)
    mix_hi = spread.astype(BF16)
    mix_lo = (spread - mix_hi.astype(F32)).astype(BF16)

    for copy in copies:
        copy.wait()

    @pl.loop(0, ncp)
    def _(cp):
        for rt in range(nrt):
            base = rt * ROWS8 * line_stride + cp
            for t in range(ntr):
                stock_a[cp, rt, t] = raw[pl.ds(base + t * ncp, ROWS8, stride=line_stride), :]
            depth = raw[pl.ds(base + ntr * ncp, ROWS8, stride=line_stride), :]
            wet[cp, rt] = (level_f < depth).astype(F32)

    first_row = lax.axis_index("grp") * rows - halo
    total_rows = rows * lax.axis_size("grp")

    def ocean_step(old, new, stock):
        @pl.loop(0, ncp)
        def _(cp):
            for rt in range(nrt):
                density = (haline * old[cp, rt, 3] - thermal * old[cp, rt, 2]) * wet[cp, rt]
                press[cp, rt] = gravity * running_sum(density)

        @pl.loop(0, ncp)
        def _(cp):
            @pl.loop(0, nrt)
            def _(rt):
                w = five(wet, cp, rt)
                open_e, open_w, open_n, open_s = (w[0] * w[k] for k in range(1, 5))
                u = five(old, cp, rt, 0)
                v = five(old, cp, rt, 1)
                temp = five(old, cp, rt, 2)
                salt = five(old, cp, rt, 3)
                p = five(press, cp, rt)
                fe = 0.5 * (u[0] + u[1]) * open_e
                fw = 0.5 * (u[0] + u[2]) * open_w
                fn = 0.5 * (v[0] + v[3]) * open_n
                fs = 0.5 * (v[0] + v[4]) * open_s
                slope_x = 0.5 * (open_e * (p[1] - p[0]) + open_w * (p[0] - p[2]))
                slope_y = 0.5 * (open_n * (p[3] - p[0]) + open_s * (p[0] - p[4]))
                row = (first_row + rt * ROWS8 + sub).astype(F32)
                f = coriolis + coriolis_slope * ((row + 0.5) / total_rows - 0.5)
                extinct = water_extinction + pigment_extinction * stock[cp, rt, 0]
                irradiance = jnp.exp(-(running_sum(extinct) - 0.5 * extinct))
                heating = heating_rate * extinct * irradiance

                def lap(q):
                    return open_e * (q[1] - q[0]) + open_w * (q[2] - q[0]) + open_n * (q[3] - q[0]) + open_s * (q[4] - q[0])

                we = -courant * jnp.minimum(fe, 0.0)
                ww = courant * jnp.maximum(fw, 0.0)
                wn = -courant * jnp.minimum(fn, 0.0)
                ws = courant * jnp.maximum(fs, 0.0)
                wc = 1.0 - courant * (
                    jnp.maximum(fe, 0.0) - jnp.minimum(fw, 0.0) + jnp.maximum(fn, 0.0) - jnp.minimum(fs, 0.0)
                )

                def carried(q):
                    return wc * q[0] + we * q[1] + ww * q[2] + wn * q[3] + ws * q[4]

                weights[cp, rt, 0] = wc
                weights[cp, rt, 1] = jnp.where(left, we, ww)
                weights[cp, rt, 2] = jnp.where(left, ww, we)
                weights[cp, rt, 3] = wn
                weights[cp, rt, 4] = ws
                new[cp, rt, 0] = (u[0] + time_step * (f * v[0] - slope_x) + viscosity * lap(u)) * w[0]
                new[cp, rt, 1] = (v[0] + time_step * (-f * u[0] - slope_y) + viscosity * lap(v)) * w[0]
                warm = (carried(temp) + diffusion * lap(temp) + heating) * w[0]
                new[cp, rt, 2] = warm
                new[cp, rt, 3] = (carried(salt) + diffusion * lap(salt)) * w[0]
                growth0[cp, rt] = reaction * jnp.exp(warming * warm) * w[0]

    def tile_step(old, cp, rt):
        wc, wx, wz, wn, ws = (weights[cp, rt, k] for k in range(5))
        advected = []
        saturated = []
        for t in range(ntr):
            c, x, z, n, s = around(old, cp, rt, t)
            a = wc * c + wx * x + wz * z + wn * n + ws * s
            advected.append(a)
            saturated.append(a / (saturation + jnp.abs(a)))
        extinct = water_extinction + pigment_extinction * advected[0]
        irradiance = jnp.exp(-(running_sum(extinct) - 0.5 * extinct))
        growth = irradiance / (irradiance + light_half) * growth0[cp, rt]
        return advected, jnp.concatenate(saturated, axis=0), growth

    def substep(old, first, last, put):
        @pl.loop(0, (last - first) // 2)
        def _(k):
            cp = first + 2 * k

            @pl.loop(0, nrt)
            def _(rt):
                a0, s0, g0 = tile_step(old, cp, rt)
                a1, s1, g1 = tile_step(old, cp + 1, rt)
                s = jnp.concatenate([s0, s1], axis=1)
                s_hi = s.astype(BF16)
                s_lo = (s - s_hi.astype(F32)).astype(BF16)
                mixed = (
                    jnp.dot(mix_hi, s_hi, preferred_element_type=F32)
                    + jnp.dot(mix_hi, s_lo, preferred_element_type=F32)
                    + jnp.dot(mix_lo, s_hi, preferred_element_type=F32)
                )
                for t in range(ntr):
                    block = mixed[t * ROWS8:(t + 1) * ROWS8]
                    put(cp, rt, t, a0[t] + g0 * block[:, :LANES])
                    put(cp + 1, rt, t, a1[t] + g1 * block[:, LANES:])

    def put_in(ref):
        def put(cp, rt, t, value):
            ref[cp, rt, t] = value

        return put

    def put_out(cp, rt, t, value):
        start = rt * ROWS8 * (ntr * inner) + t * inner + (cp - halo // 2)
        result[pl.ds(start, ROWS8, stride=ntr * inner), :] = value

    edge = halo // 2
    ocean_step(ocean_a, ocean_b, stock_a)
    substep(stock_a, 0, ncp, put_in(stock_b))
    substep(stock_b, 0, ncp, put_in(stock_a))
    ocean_step(ocean_b, ocean_a, stock_a)
    substep(stock_a, 0, ncp, put_in(stock_b))
    substep(stock_b, edge, ncp - edge, put_out)
    send = pltpu.make_async_copy(result.at[pl.ds(halo * ntr * inner, rows * ntr * inner)], out, sem.at[0])
    send.start()
    for f in range(4):
        for cp in range(inner):
            for rt in range(nrt):
                sea[f, pl.ds(rt * ROWS8, ROWS8), pl.ds(cp * LANES, LANES)] = ocean_a[cp + edge, rt, f]
        ocean_out[f] = sea[f, pl.ds(halo, rows), pl.ds(0, inner * LANES)]
    send.wait()


def run_window(tile, south, north, ocean, ocean_south, ocean_north, interaction, ntr, ncp):
    rows = ocean.shape[1]
    halo = HALO
    nrt = (rows + 2 * halo) // ROWS8
    inner = ncp - halo
    anywhere = pl.BlockSpec(memory_space=pl.ANY)
    inside = pl.BlockSpec(memory_space=pltpu.VMEM)
    return pl.pallas_call(
        main_kernel,
        out_shape=(
            jax.ShapeDtypeStruct((4, rows, inner * LANES), F32),
            jax.ShapeDtypeStruct((rows * ntr * inner, LANES), F32),
        ),
        in_specs=[anywhere] * 3 + [inside] * 4,
        out_specs=(inside, anywhere),
        scratch_shapes=[
            pltpu.VMEM(((rows + 2 * halo) * (ntr + 1) * ncp, LANES), F32),
            pltpu.VMEM((ncp, nrt, ntr, ROWS8, LANES), F32),
            pltpu.VMEM((ncp, nrt, ntr, ROWS8, LANES), F32),
            pltpu.VMEM((4, rows + 2 * halo, ncp * LANES), F32),
            pltpu.VMEM((ncp, nrt, 4, ROWS8, LANES), F32),
            pltpu.VMEM((ncp, nrt, 4, ROWS8, LANES), F32),
            pltpu.VMEM((ncp, nrt, ROWS8, LANES), F32),
            pltpu.VMEM((ncp, nrt, ROWS8, LANES), F32),
            pltpu.VMEM((ncp, nrt, 5, ROWS8, LANES), F32),
            pltpu.VMEM((ncp, nrt, ROWS8, LANES), F32),
            pltpu.VMEM(((rows + 2 * halo) * ntr * inner, LANES), F32),
            pltpu.SemaphoreType.DMA((3,)),
        ],
        name="window",
    )(tile, south, north, ocean, ocean_south, ocean_north, interaction)


def shift(array, axis, by):
    count = lax.axis_size(axis)
    if by > 0:
        return lax.ppermute(array, axis, [(i, i + 1) for i in range(count - 1)])
    return lax.ppermute(array, axis, [(i + 1, i) for i in range(count - 1)])


def shards(ocean_fields, tracers, wet_levels, interaction):
    tiles = lax.axis_size("gx")
    ntr = tracers.shape[0]
    rows = ocean_fields.shape[1]
    columns = wet_levels.shape[1]
    levels = tracers.shape[2] // columns
    lines = tracers.shape[2] // LANES
    pair = LANES // levels
    inner = lines // tiles
    edge = HALO // pair
    ncp = inner + 2 * edge
    planes = ntr + 1

    margin = edge * LANES
    from_west = shift(ocean_fields[:, :, -margin:], "gx", 1)
    from_east = shift(ocean_fields[:, :, :margin], "gx", -1)
    depth = jnp.broadcast_to(wet_levels.astype(F32).reshape(lines, pair, 1), (lines, pair, levels))
    sent = cut_windows(tracers.reshape(ntr, lines, 1, LANES), depth.reshape(1, lines, 1, LANES), tiles, ncp)
    ocean = jnp.concatenate([from_west, ocean_fields, from_east], axis=2)
    ocean_south = shift(ocean[:, -HALO:], "grp", 1)
    ocean_north = shift(ocean[:, :HALO], "grp", -1)
    sent, ocean, ocean_south, ocean_north = lax.optimization_barrier((sent, ocean, ocean_south, ocean_north))
    tile = lax.all_to_all(sent.reshape(tiles, planes * ncp, LANES), "gx", split_axis=0, concat_axis=0, tiled=True)
    south = shift(tile[-HALO:], "grp", 1)
    north = shift(tile[:HALO], "grp", -1)
    ocean_next, result = run_window(
        tile.reshape(-1, LANES), south.reshape(-1, LANES), north.reshape(-1, LANES),
        ocean, ocean_south, ocean_north, interaction, ntr, ncp,
    )
    back = lax.all_to_all(result.reshape(tiles, ntr * inner, LANES), "gx", split_axis=0, concat_axis=0, tiled=True)
    back = back.reshape(tiles, ntr, inner, LANES).transpose(1, 0, 2, 3)
    return ocean_next, back.reshape(ntr, 1, lines * LANES)


def solution(mesh):
    placed = (P(None, "grp", "gx"), P(None, ("grp", "gx"), None), P(("grp", "gx"), None), P())
    return jax.shard_map(
        shards,
        mesh=mesh,
        in_specs=placed,
        out_specs=(P(None, "grp", "gx"), P(None, ("grp", "gx"), None)),
        check_vma=False,
    )
```

```python
import jax
import jax.numpy as jnp
from jax import lax
from jax.experimental import pallas as pl
from jax.experimental.pallas import tpu as pltpu
from jax.sharding import PartitionSpec as P

NC = 2
NB = 2
HALO = NC * NB

courant = 0.2
diffusion = 0.08
viscosity = 0.08
time_step = 0.1
thermal = 0.2
haline = 0.15
gravity = 0.1
coriolis = 0.5
coriolis_slope = 0.5
water_extinction = 0.04
pigment_extinction = 0.01
heating_rate = 0.5
light_half = 0.3
warming = 0.1
saturation = 0.5
reaction = 0.5

LANES = 128
ROWS8 = 8
F32 = jnp.float32
BF16 = jnp.bfloat16


def window_kernel(strip, depth_plane, out, big, sem_in, sem_out):
    planes, lines = big.shape[0], strip.shape[1]
    tiles, wide = out.shape[0], out.shape[2]
    step = lines // tiles
    edge = (wide - step) // 2
    tracers_in = pltpu.make_async_copy(strip, big.at[pl.ds(0, planes - 1), pl.ds(edge, lines)], sem_in.at[0])
    depth_in = pltpu.make_async_copy(depth_plane, big.at[pl.ds(planes - 1, 1), pl.ds(edge, lines)], sem_in.at[1])
    tracers_in.start()
    depth_in.start()
    zeros = jnp.zeros((planes, edge, 1, LANES), F32)
    big[:, pl.ds(0, edge)] = zeros
    big[:, pl.ds(edge + lines, edge)] = zeros
    tracers_in.wait()
    depth_in.wait()

    def send(d):
        return pltpu.make_async_copy(big.at[:, pl.ds(d * step, wide)], out.at[d], sem_out.at[d])

    @pl.loop(0, tiles)
    def _(d):
        send(d).start()

    @pl.loop(0, tiles)
    def _(d):
        send(d).wait()


def cut_windows(strip, depth_plane, tiles, wide):
    planes = strip.shape[0] + 1
    lines = strip.shape[1]
    edge = (wide - lines // tiles) // 2
    anywhere = pl.BlockSpec(memory_space=pl.ANY)
    return pl.pallas_call(
        window_kernel,
        out_shape=jax.ShapeDtypeStruct((tiles, planes, wide, 1, LANES), F32),
        in_specs=[anywhere, anywhere],
        out_specs=anywhere,
        scratch_shapes=[
            pltpu.VMEM((planes, lines + 2 * edge, 1, LANES), F32),
            pltpu.SemaphoreType.DMA((2,)),
            pltpu.SemaphoreType.DMA((tiles,)),
        ],
        name="cut_windows",
    )(strip, depth_plane)


def main_kernel(
    tile, south, north, ocean, ocean_south, ocean_north, mix_ref, ocean_out, out,
    raw, stock_a, stock_b, sea, ocean_a, ocean_b, press, wet, weights, growth0, growth, flat, result, sem,
):
    ncp, nrt, ntr = stock_a.shape[0], stock_a.shape[1] - 2, stock_a.shape[2]
    planes = ntr + 1
    line_stride = planes * ncp
    rows = tile.shape[0] // line_stride
    halo = HALO
    inner = ncp - halo
    copies = [
        pltpu.make_async_copy(south, raw.at[pl.ds(0, halo * line_stride)], sem.at[0]),
        pltpu.make_async_copy(tile, raw.at[pl.ds(halo * line_stride, rows * line_stride)], sem.at[1]),
        pltpu.make_async_copy(north, raw.at[pl.ds((halo + rows) * line_stride, halo * line_stride)], sem.at[2]),
    ]
    for copy in copies:
        copy.start()

    lane = lax.broadcasted_iota(jnp.int32, (ROWS8, LANES), 1)
    sub = lax.broadcasted_iota(jnp.int32, (ROWS8, LANES), 0)
    half = LANES // 2
    left = lane < half
    level_f = (lane % half).astype(F32)

    def swap(x):
        return pltpu.roll(x, half, 1)

    def put(ref, cp, q, value, *more):
        ref[(cp, q + 1, *more)] = value
        if q == 0:
            ref[(cp, nrt + 1, *more)] = pltpu.roll(value, ROWS8 - 1, 0)
        if q == nrt - 1:
            ref[(cp, 0, *more)] = pltpu.roll(value, 1, 0)

    def around(ref, cp, q, *more):
        right = ref[(jnp.minimum(cp + 1, ncp - 1), q + 1, *more)]
        leftward = ref[(jnp.maximum(cp - 1, 0), q + 1, *more)]
        centre = ref[(cp, q + 1, *more)]
        far = swap(jnp.where(left, right, leftward))
        return centre, swap(centre), far, ref[(cp, q + 2, *more)], ref[(cp, q, *more)]

    def five(ref, cp, q, *more):
        centre, swapped, far, cell_north, cell_south = around(ref, cp, q, *more)
        return centre, jnp.where(left, swapped, far), jnp.where(left, far, swapped), cell_north, cell_south

    row_id = lax.broadcasted_iota(jnp.int32, (LANES, LANES), 0)
    col_id = lax.broadcasted_iota(jnp.int32, (LANES, LANES), 1)
    upper = ((row_id <= col_id) & (row_id // half == col_id // half)).astype(F32).astype(BF16)

    def running_sums(x):
        high = x.astype(BF16)
        rest = x - high.astype(F32)
        middle = rest.astype(BF16)
        low = (rest - middle.astype(F32)).astype(BF16)
        return (
            jnp.dot(high, upper, preferred_element_type=F32)
            + jnp.dot(middle, upper, preferred_element_type=F32)
            + jnp.dot(low, upper, preferred_element_type=F32)
        )

    for f in range(4):
        for cp in range(ncp):
            across = pl.ds(cp * LANES, LANES)
            sea[f, cp, pl.ds(0, halo), :] = ocean_south[f, :, across]
            sea[f, cp, pl.ds(halo, rows), :] = ocean[f, :, across]
            sea[f, cp, pl.ds(halo + rows, halo), :] = ocean_north[f, :, across]
            for q in range(nrt):
                put(ocean_a, cp, q, sea[f, cp, pl.ds(q, ROWS8, stride=nrt), :], f)

    wide = ntr * ROWS8
    pick = (lax.broadcasted_iota(jnp.int32, (wide, ntr), 0) // ROWS8 == lax.broadcasted_iota(jnp.int32, (wide, ntr), 1)).astype(F32)
    deep = (ntr + 1) * ROWS8
    pick_t = (lax.broadcasted_iota(jnp.int32, (ntr, deep), 1) // ROWS8 == lax.broadcasted_iota(jnp.int32, (ntr, deep), 0)).astype(F32)
    spread = jnp.dot(
        jnp.dot(pick, mix_ref[...], precision=lax.Precision.HIGHEST, preferred_element_type=F32),
        pick_t, precision=lax.Precision.HIGHEST, preferred_element_type=F32,
    )
    same = lax.broadcasted_iota(jnp.int32, (wide, deep), 0) % ROWS8 == lax.broadcasted_iota(jnp.int32, (wide, deep), 1) % ROWS8
    spread = jnp.where(same, spread, 0.0)
    mix_hi = spread.astype(BF16).astype(F32)
    mix_all = jnp.concatenate([mix_hi, mix_hi, spread - mix_hi], axis=1).astype(BF16)

    for copy in copies:
        copy.wait()

    @pl.loop(0, ncp)
    def _(cp):
        for q in range(nrt):
            base = q * line_stride + cp
            for t in range(ntr):
                put(stock_a, cp, q, raw[pl.ds(base + t * ncp, ROWS8, stride=nrt * line_stride), :], t)
            depth = raw[pl.ds(base + ntr * ncp, ROWS8, stride=nrt * line_stride), :]
            put(wet, cp, q, (level_f < depth).astype(F32))

    first_row = lax.axis_index("grp") * rows - halo
    total_rows = rows * lax.axis_size("grp")

    def line(cp, q):
        return pl.ds((cp * nrt + q) * ROWS8, ROWS8)

    def ocean_step(old, new, stock):
        for cp in range(ncp):
            for q in range(nrt):
                flat[line(cp, q), :] = (haline * old[cp, q + 1, 3] - thermal * old[cp, q + 1, 2]) * wet[cp, q + 1]
        flat[...] = gravity * running_sums(flat[...])
        for cp in range(ncp):
            for q in range(nrt):
                put(press, cp, q, flat[line(cp, q), :])
        for cp in range(ncp):
            for q in range(nrt):
                flat[line(cp, q), :] = water_extinction + pigment_extinction * stock[cp, q + 1, 0]
        extinct_all = flat[...]
        flat[...] = heating_rate * extinct_all * jnp.exp(-(running_sums(extinct_all) - 0.5 * extinct_all))

        @pl.loop(0, ncp)
        def _(cp):
            for q in range(nrt):
                w = five(wet, cp, q)
                open_e, open_w, open_n, open_s = (w[0] * w[k] for k in range(1, 5))
                u = five(old, cp, q, 0)
                v = five(old, cp, q, 1)
                temp = five(old, cp, q, 2)
                salt = five(old, cp, q, 3)
                p = five(press, cp, q)
                fe = 0.5 * (u[0] + u[1]) * open_e
                fw = 0.5 * (u[0] + u[2]) * open_w
                fn = 0.5 * (v[0] + v[3]) * open_n
                fs = 0.5 * (v[0] + v[4]) * open_s
                slope_x = 0.5 * (open_e * (p[1] - p[0]) + open_w * (p[0] - p[2]))
                slope_y = 0.5 * (open_n * (p[3] - p[0]) + open_s * (p[0] - p[4]))
                row = (first_row + q + nrt * sub).astype(F32)
                f = coriolis + coriolis_slope * ((row + 0.5) / total_rows - 0.5)
                heating = flat[pl.ds(pl.multiple_of((cp * nrt + q) * ROWS8, ROWS8), ROWS8), :]

                def lap(x):
                    return open_e * (x[1] - x[0]) + open_w * (x[2] - x[0]) + open_n * (x[3] - x[0]) + open_s * (x[4] - x[0])

                we = -courant * jnp.minimum(fe, 0.0)
                ww = courant * jnp.maximum(fw, 0.0)
                wn = -courant * jnp.minimum(fn, 0.0)
                ws = courant * jnp.maximum(fs, 0.0)
                wc = 1.0 - courant * (
                    jnp.maximum(fe, 0.0) - jnp.minimum(fw, 0.0) + jnp.maximum(fn, 0.0) - jnp.minimum(fs, 0.0)
                )

                def carried(x):
                    return wc * x[0] + we * x[1] + ww * x[2] + wn * x[3] + ws * x[4]

                weights[cp, q, 0] = wc
                weights[cp, q, 1] = jnp.where(left, we, ww)
                weights[cp, q, 2] = jnp.where(left, ww, we)
                weights[cp, q, 3] = wn
                weights[cp, q, 4] = ws
                put(new, cp, q, (u[0] + time_step * (f * v[0] - slope_x) + viscosity * lap(u)) * w[0], 0)
                put(new, cp, q, (v[0] + time_step * (-f * u[0] - slope_y) + viscosity * lap(v)) * w[0], 1)
                warm = (carried(temp) + diffusion * lap(temp) + heating) * w[0]
                put(new, cp, q, warm, 2)
                put(new, cp, q, (carried(salt) + diffusion * lap(salt)) * w[0], 3)
                growth0[cp, q] = reaction * jnp.exp(warming * warm) * w[0]

    def carry(old, cp, q, t, weight):
        c, x, z, n, s = around(old, cp, q, t)
        return weight[0] * c + weight[1] * x + weight[2] * z + weight[3] * n + weight[4] * s

    def substep(old, first, last, finish):
        for cp in range(first, last):
            for q in range(nrt):
                p = carry(old, cp, q, 0, [weights[cp, q, k] for k in range(5)])
                flat[line(cp, q), :] = water_extinction + pigment_extinction * p
        span = pl.ds(first * nrt * ROWS8, (last - first) * nrt * ROWS8)
        extinct = flat[span, :]
        irradiance = jnp.exp(-(running_sums(extinct) - 0.5 * extinct))
        flat[span, :] = irradiance / (irradiance + light_half)
        for cp in range(first, last):
            for q in range(nrt):
                growth[cp, q] = flat[line(cp, q), :] * growth0[cp, q]

        blank = jnp.zeros((ROWS8, LANES), F32)

        @pl.loop(first, last)
        def _(cp):
            def begin(q):
                weight = [weights[cp, q, k] for k in range(5)]
                advected, high, low = [], [], []
                for t in range(ntr):
                    a = carry(old, cp, q, t, weight)
                    s = a / (saturation + jnp.abs(a))
                    h = s.astype(BF16).astype(F32)
                    advected.append(a)
                    high.append(h)
                    low.append(s - h)
                high = jnp.concatenate(high + [blank], axis=0).astype(BF16)
                low = jnp.concatenate(low + [blank], axis=0).astype(BF16)
                return advected, jnp.concatenate([high, low, high], axis=0)

            def end(group, begun):
                parts = [b[1] for b in begun]
                s = parts[0] if len(parts) == 1 else jnp.concatenate(parts, axis=1)
                mixed = jnp.dot(mix_all, s, preferred_element_type=F32)
                for k, q in enumerate(group):
                    g = growth[cp, q]
                    for t in range(ntr):
                        block = mixed[t * ROWS8:(t + 1) * ROWS8, k * LANES:(k + 1) * LANES]
                        finish(cp, q, t, begun[k][0][t] + g * block)

            for q in range(0, nrt, 2):
                group = list(range(q, min(q + 2, nrt)))
                end(group, [begin(r) for r in group])

    def finish_in(ref):
        def finish(cp, q, t, value):
            put(ref, cp, q, value, t)

        return finish

    def finish_out(cp, q, t, value):
        start = q * (ntr * inner) + t * inner + (cp - halo // 2)
        result[pl.ds(start, ROWS8, stride=nrt * ntr * inner), :] = value

    edge = halo // 2
    ocean_step(ocean_a, ocean_b, stock_a)
    substep(stock_a, 0, ncp, finish_in(stock_b))
    substep(stock_b, edge // 2, ncp - edge // 2, finish_in(stock_a))
    ocean_step(ocean_b, ocean_a, stock_a)
    substep(stock_a, edge // 2, ncp - edge // 2, finish_in(stock_b))
    substep(stock_b, edge, ncp - edge, finish_out)
    send = pltpu.make_async_copy(result.at[pl.ds(halo * ntr * inner, rows * ntr * inner)], out, sem.at[0])
    send.start()
    for f in range(4):
        for cp in range(inner):
            for q in range(nrt):
                sea[f, cp, pl.ds(q, ROWS8, stride=nrt), :] = ocean_a[cp + edge, q + 1, f]
            ocean_out[f, :, pl.ds(cp * LANES, LANES)] = sea[f, cp, pl.ds(halo, rows), :]
    send.wait()


def run_window(tile, south, north, ocean, ocean_south, ocean_north, interaction, ntr, ncp):
    rows = ocean.shape[1]
    halo = HALO
    nrt = (rows + 2 * halo) // ROWS8
    inner = ncp - halo
    anywhere = pl.BlockSpec(memory_space=pl.ANY)
    inside = pl.BlockSpec(memory_space=pltpu.VMEM)
    return pl.pallas_call(
        main_kernel,
        out_shape=(
            jax.ShapeDtypeStruct((4, rows, inner * LANES), F32),
            jax.ShapeDtypeStruct((rows * ntr * inner, LANES), F32),
        ),
        in_specs=[anywhere] * 3 + [inside] * 4,
        out_specs=(inside, anywhere),
        scratch_shapes=[
            pltpu.VMEM(((rows + 2 * halo) * (ntr + 1) * ncp, LANES), F32),
            pltpu.VMEM((ncp, nrt + 2, ntr, ROWS8, LANES), F32),
            pltpu.VMEM((ncp, nrt + 2, ntr, ROWS8, LANES), F32),
            pltpu.VMEM((4, ncp, rows + 2 * halo, LANES), F32),
            pltpu.VMEM((ncp, nrt + 2, 4, ROWS8, LANES), F32),
            pltpu.VMEM((ncp, nrt + 2, 4, ROWS8, LANES), F32),
            pltpu.VMEM((ncp, nrt + 2, ROWS8, LANES), F32),
            pltpu.VMEM((ncp, nrt + 2, ROWS8, LANES), F32),
            pltpu.VMEM((ncp, nrt, 5, ROWS8, LANES), F32),
            pltpu.VMEM((ncp, nrt, ROWS8, LANES), F32),
            pltpu.VMEM((ncp, nrt, ROWS8, LANES), F32),
            pltpu.VMEM((ncp * nrt * ROWS8, LANES), F32),
            pltpu.VMEM(((rows + 2 * halo) * ntr * inner, LANES), F32),
            pltpu.SemaphoreType.DMA((3,)),
        ],
        name="window",
    )(tile, south, north, ocean, ocean_south, ocean_north, interaction)


def shift(array, axis, by):
    count = lax.axis_size(axis)
    if by > 0:
        return lax.ppermute(array, axis, [(i, i + 1) for i in range(count - 1)])
    return lax.ppermute(array, axis, [(i + 1, i) for i in range(count - 1)])


def shards(ocean_fields, tracers, wet_levels, interaction):
    tiles = lax.axis_size("gx")
    ntr = tracers.shape[0]
    rows = ocean_fields.shape[1]
    columns = wet_levels.shape[1]
    levels = tracers.shape[2] // columns
    lines = tracers.shape[2] // LANES
    pair = LANES // levels
    inner = lines // tiles
    edge = HALO // pair
    ncp = inner + 2 * edge
    planes = ntr + 1

    margin = edge * LANES
    from_west = shift(ocean_fields[:, :, -margin:], "gx", 1)
    from_east = shift(ocean_fields[:, :, :margin], "gx", -1)
    depth = jnp.broadcast_to(wet_levels.astype(F32).reshape(lines, pair, 1), (lines, pair, levels))
    sent = cut_windows(tracers.reshape(ntr, lines, 1, LANES), depth.reshape(1, lines, 1, LANES), tiles, ncp)
    ocean = jnp.concatenate([from_west, ocean_fields, from_east], axis=2)
    ocean_south = shift(ocean[:, -HALO:], "grp", 1)
    ocean_north = shift(ocean[:, :HALO], "grp", -1)
    sent, ocean, ocean_south, ocean_north = lax.optimization_barrier((sent, ocean, ocean_south, ocean_north))
    tile = lax.all_to_all(sent.reshape(tiles, planes * ncp, LANES), "gx", split_axis=0, concat_axis=0, tiled=True)
    south = shift(tile[-HALO:], "grp", 1)
    north = shift(tile[:HALO], "grp", -1)
    ocean_next, result = run_window(
        tile.reshape(-1, LANES), south.reshape(-1, LANES), north.reshape(-1, LANES),
        ocean, ocean_south, ocean_north, interaction, ntr, ncp,
    )
    back = lax.all_to_all(result.reshape(tiles, ntr * inner, LANES), "gx", split_axis=0, concat_axis=0, tiled=True)
    back = back.reshape(tiles, ntr, inner, LANES).transpose(1, 0, 2, 3)
    return ocean_next, back.reshape(ntr, 1, lines * LANES)


def solution(mesh):
    placed = (P(None, "grp", "gx"), P(None, ("grp", "gx"), None), P(("grp", "gx"), None), P())
    return jax.shard_map(
        shards,
        mesh=mesh,
        in_specs=placed,
        out_specs=(P(None, "grp", "gx"), P(None, ("grp", "gx"), None)),
        check_vma=False,
    )
```

```python
import jax
import jax.numpy as jnp
from jax import lax
from jax.experimental import pallas as pl
from jax.experimental.pallas import tpu as pltpu
from jax.sharding import PartitionSpec as P

NC = 2
NB = 2
HALO = NC * NB

courant = 0.2
diffusion = 0.08
viscosity = 0.08
time_step = 0.1
thermal = 0.2
haline = 0.15
gravity = 0.1
coriolis = 0.5
coriolis_slope = 0.5
water_extinction = 0.04
pigment_extinction = 0.01
heating_rate = 0.5
light_half = 0.3
warming = 0.1
saturation = 0.5
reaction = 0.5

LANES = 128
ROWS8 = 8
F32 = jnp.float32
BF16 = jnp.bfloat16


def window_kernel(strip, depth_plane, out, big, sem_in, sem_out):
    planes, lines = big.shape[0], strip.shape[1]
    tiles, wide = out.shape[0], out.shape[2]
    step = lines // tiles
    edge = (wide - step) // 2
    tracers_in = pltpu.make_async_copy(strip, big.at[pl.ds(0, planes - 1), pl.ds(edge, lines)], sem_in.at[0])
    depth_in = pltpu.make_async_copy(depth_plane, big.at[pl.ds(planes - 1, 1), pl.ds(edge, lines)], sem_in.at[1])
    tracers_in.start()
    depth_in.start()
    zeros = jnp.zeros((planes, edge, 1, LANES), F32)
    big[:, pl.ds(0, edge)] = zeros
    big[:, pl.ds(edge + lines, edge)] = zeros
    tracers_in.wait()
    depth_in.wait()

    def send(d):
        return pltpu.make_async_copy(big.at[:, pl.ds(d * step, wide)], out.at[d], sem_out.at[d])

    @pl.loop(0, tiles)
    def _(d):
        send(d).start()

    @pl.loop(0, tiles)
    def _(d):
        send(d).wait()


def cut_windows(strip, depth_plane, tiles, wide):
    planes = strip.shape[0] + 1
    lines = strip.shape[1]
    edge = (wide - lines // tiles) // 2
    anywhere = pl.BlockSpec(memory_space=pl.ANY)
    return pl.pallas_call(
        window_kernel,
        out_shape=jax.ShapeDtypeStruct((tiles, planes, wide, 1, LANES), F32),
        in_specs=[anywhere, anywhere],
        out_specs=pl.BlockSpec(memory_space=pltpu.HBM),
        scratch_shapes=[
            pltpu.VMEM((planes, lines + 2 * edge, 1, LANES), F32),
            pltpu.SemaphoreType.DMA((2,)),
            pltpu.SemaphoreType.DMA((tiles,)),
        ],
        compiler_params=pltpu.CompilerParams(vmem_limit_bytes=16 * 2**20),
        name="cut_windows",
    )(strip, depth_plane)


def edge_kernel(tile, west, ocean, east, to_north, to_south, lines, sem):
    planes_lines = tile.shape[1]
    rows = ocean.shape[1]
    halo = HALO
    wide = lines.shape[1] // halo
    sides = ((to_north, rows - halo), (to_south, 0))
    copies = [
        pltpu.make_async_copy(
            tile.at[first + r],
            message.at[pl.ds(r * (planes_lines + wide), planes_lines)],
            sem.at[k * halo + r],
        )
        for k, (message, first) in enumerate(sides)
        for r in range(halo)
    ]
    for copy in copies:
        copy.start()
    for k, (message, first) in enumerate(sides):
        c = 0
        for f in range(4):
            for part in (west, ocean, east):
                for j in range(part.shape[2] // LANES):
                    lines[k, pl.ds(c, halo, stride=wide), :] = part[f, pl.ds(first, halo), pl.ds(j * LANES, LANES)]
                    c += 1
    more = [
        pltpu.make_async_copy(
            lines.at[k, pl.ds(r * wide, wide)],
            message.at[pl.ds(r * (planes_lines + wide) + planes_lines, wide)],
            sem.at[(2 + k) * halo + r],
        )
        for k, (message, first) in enumerate(sides)
        for r in range(halo)
    ]
    for copy in more:
        copy.start()
    for copy in copies + more:
        copy.wait()


def row_messages(tile, west, ocean, east, ncp):
    anywhere = pl.BlockSpec(memory_space=pl.ANY)
    inside = pl.BlockSpec(memory_space=pltpu.VMEM)
    message = jax.ShapeDtypeStruct((HALO * (tile.shape[1] + 4 * ncp), LANES), F32)
    return pl.pallas_call(
        edge_kernel,
        out_shape=(message, message),
        in_specs=[anywhere, inside, inside, inside],
        out_specs=(anywhere, anywhere),
        scratch_shapes=[
            pltpu.VMEM((2, HALO * 4 * ncp, LANES), F32),
            pltpu.SemaphoreType.DMA((4 * HALO,)),
        ],
        compiler_params=pltpu.CompilerParams(vmem_limit_bytes=8 * 2**20),
        name="row_messages",
    )(tile, west, ocean, east)


def main_kernel(
    tile, south, north, west, ocean, east, mix_ref, ocean_out, out,
    raw, stock_a, stock_b, sea, beyond, ocean_a, ocean_b, press, wet, weights, growth0, growth, flat, result, sem,
):
    ncp, nrt, ntr = stock_a.shape[0], stock_a.shape[1] - 2, stock_a.shape[2]
    planes = ntr + 1
    line_stride = planes * ncp
    rows = tile.shape[0] // line_stride
    halo = HALO
    inner = ncp - halo
    wide_ocean = 4 * ncp
    copies = [
        pltpu.make_async_copy(tile, raw.at[pl.ds(halo * line_stride, rows * line_stride)], sem.at[0]),
    ]
    for side, message in enumerate((south, north)):
        for r in range(halo):
            start = r * (line_stride + wide_ocean)
            row = r + side * (halo + rows)
            copies.append(pltpu.make_async_copy(
                message.at[pl.ds(start, line_stride)], raw.at[pl.ds(row * line_stride, line_stride)],
                sem.at[len(copies)],
            ))
            copies.append(pltpu.make_async_copy(
                message.at[pl.ds(start + line_stride, wide_ocean)], beyond.at[side, pl.ds(r * wide_ocean, wide_ocean)],
                sem.at[len(copies)],
            ))
    for copy in copies:
        copy.start()

    lane = lax.broadcasted_iota(jnp.int32, (ROWS8, LANES), 1)
    sub = lax.broadcasted_iota(jnp.int32, (ROWS8, LANES), 0)
    half = LANES // 2
    left = lane < half
    level_f = (lane % half).astype(F32)

    def swap(x):
        return pltpu.roll(x, half, 1)

    def put(ref, cp, q, value, *more):
        ref[(cp, q + 1, *more)] = value
        if q == 0:
            ref[(cp, nrt + 1, *more)] = pltpu.roll(value, ROWS8 - 1, 0)
        if q == nrt - 1:
            ref[(cp, 0, *more)] = pltpu.roll(value, 1, 0)

    def around(ref, cp, q, *more):
        right = ref[(jnp.minimum(cp + 1, ncp - 1), q + 1, *more)]
        leftward = ref[(jnp.maximum(cp - 1, 0), q + 1, *more)]
        centre = ref[(cp, q + 1, *more)]
        far = swap(jnp.where(left, right, leftward))
        return centre, swap(centre), far, ref[(cp, q + 2, *more)], ref[(cp, q, *more)]

    def five(ref, cp, q, *more):
        centre, swapped, far, cell_north, cell_south = around(ref, cp, q, *more)
        return centre, jnp.where(left, swapped, far), jnp.where(left, far, swapped), cell_north, cell_south

    row_id = lax.broadcasted_iota(jnp.int32, (LANES, LANES), 0)
    col_id = lax.broadcasted_iota(jnp.int32, (LANES, LANES), 1)
    upper = ((row_id <= col_id) & (row_id // half == col_id // half)).astype(F32).astype(BF16)

    def running_sums(x):
        high = x.astype(BF16)
        rest = x - high.astype(F32)
        middle = rest.astype(BF16)
        low = (rest - middle.astype(F32)).astype(BF16)
        return (
            jnp.dot(high, upper, preferred_element_type=F32)
            + jnp.dot(middle, upper, preferred_element_type=F32)
            + jnp.dot(low, upper, preferred_element_type=F32)
        )

    wide = ntr * ROWS8
    deep = (ntr + 1) * ROWS8
    pick = (lax.broadcasted_iota(jnp.int32, (wide, ntr), 0) // ROWS8 == lax.broadcasted_iota(jnp.int32, (wide, ntr), 1)).astype(F32).astype(BF16)
    pick_t = (lax.broadcasted_iota(jnp.int32, (ntr, deep), 1) // ROWS8 == lax.broadcasted_iota(jnp.int32, (ntr, deep), 0)).astype(F32).astype(BF16)
    same = lax.broadcasted_iota(jnp.int32, (wide, deep), 0) % ROWS8 == lax.broadcasted_iota(jnp.int32, (wide, deep), 1) % ROWS8

    def spread(part):
        tall = jnp.dot(pick, part, preferred_element_type=F32).astype(BF16)
        return jnp.where(same, jnp.dot(tall, pick_t, preferred_element_type=F32), 0.0)

    mix = mix_ref[...]
    mix_hi = mix.astype(BF16)
    mix_lo = (mix - mix_hi.astype(F32)).astype(BF16)
    spread_hi = spread(mix_hi)
    mix_all = jnp.concatenate([spread_hi, spread_hi, spread(mix_lo)], axis=1).astype(BF16)

    for copy in copies:
        copy.wait()

    for f in range(4):
        for cp in range(ncp):
            if cp < halo // 2:
                part, j = west, cp
            elif cp < ncp - halo // 2:
                part, j = ocean, cp - halo // 2
            else:
                part, j = east, cp - (ncp - halo // 2)
            sea[f, cp, pl.ds(0, halo), :] = beyond[0, pl.ds(f * ncp + cp, halo, stride=wide_ocean), :]
            sea[f, cp, pl.ds(halo, rows), :] = part[f, :, pl.ds(j * LANES, LANES)]
            sea[f, cp, pl.ds(halo + rows, halo), :] = beyond[1, pl.ds(f * ncp + cp, halo, stride=wide_ocean), :]
            for q in range(nrt):
                put(ocean_a, cp, q, sea[f, cp, pl.ds(q, ROWS8, stride=nrt), :], f)

    @pl.loop(0, ncp)
    def _(cp):
        for q in range(nrt):
            base = q * line_stride + cp
            for t in range(ntr):
                put(stock_a, cp, q, raw[pl.ds(base + t * ncp, ROWS8, stride=nrt * line_stride), :], t)
            depth = raw[pl.ds(base + ntr * ncp, ROWS8, stride=nrt * line_stride), :]
            put(wet, cp, q, (level_f < depth).astype(F32))

    first_row = lax.axis_index("grp") * rows - halo
    total_rows = rows * lax.axis_size("grp")

    def line(cp, q):
        return pl.ds((cp * nrt + q) * ROWS8, ROWS8)

    def ocean_step(old, new, stock):
        for cp in range(ncp):
            for q in range(nrt):
                flat[line(cp, q), :] = (haline * old[cp, q + 1, 3] - thermal * old[cp, q + 1, 2]) * wet[cp, q + 1]
        flat[...] = gravity * running_sums(flat[...])
        for cp in range(ncp):
            for q in range(nrt):
                put(press, cp, q, flat[line(cp, q), :])
        for cp in range(ncp):
            for q in range(nrt):
                flat[line(cp, q), :] = water_extinction + pigment_extinction * stock[cp, q + 1, 0]
        extinct_all = flat[...]
        flat[...] = heating_rate * extinct_all * jnp.exp(-(running_sums(extinct_all) - 0.5 * extinct_all))

        @pl.loop(0, ncp)
        def _(cp):
            for q in range(nrt):
                w = five(wet, cp, q)
                open_e, open_w, open_n, open_s = (w[0] * w[k] for k in range(1, 5))
                u = five(old, cp, q, 0)
                v = five(old, cp, q, 1)
                temp = five(old, cp, q, 2)
                salt = five(old, cp, q, 3)
                p = five(press, cp, q)
                fe = 0.5 * (u[0] + u[1]) * open_e
                fw = 0.5 * (u[0] + u[2]) * open_w
                fn = 0.5 * (v[0] + v[3]) * open_n
                fs = 0.5 * (v[0] + v[4]) * open_s
                slope_x = 0.5 * (open_e * (p[1] - p[0]) + open_w * (p[0] - p[2]))
                slope_y = 0.5 * (open_n * (p[3] - p[0]) + open_s * (p[0] - p[4]))
                row = (first_row + q + nrt * sub).astype(F32)
                f = coriolis + coriolis_slope * ((row + 0.5) / total_rows - 0.5)
                heating = flat[pl.ds(pl.multiple_of((cp * nrt + q) * ROWS8, ROWS8), ROWS8), :]

                def lap(x):
                    return open_e * (x[1] - x[0]) + open_w * (x[2] - x[0]) + open_n * (x[3] - x[0]) + open_s * (x[4] - x[0])

                we = -courant * jnp.minimum(fe, 0.0)
                ww = courant * jnp.maximum(fw, 0.0)
                wn = -courant * jnp.minimum(fn, 0.0)
                ws = courant * jnp.maximum(fs, 0.0)
                wc = 1.0 - courant * (
                    jnp.maximum(fe, 0.0) - jnp.minimum(fw, 0.0) + jnp.maximum(fn, 0.0) - jnp.minimum(fs, 0.0)
                )

                def carried(x):
                    return wc * x[0] + we * x[1] + ww * x[2] + wn * x[3] + ws * x[4]

                weights[cp, q, 0] = wc
                weights[cp, q, 1] = jnp.where(left, we, ww)
                weights[cp, q, 2] = jnp.where(left, ww, we)
                weights[cp, q, 3] = wn
                weights[cp, q, 4] = ws
                put(new, cp, q, (u[0] + time_step * (f * v[0] - slope_x) + viscosity * lap(u)) * w[0], 0)
                put(new, cp, q, (v[0] + time_step * (-f * u[0] - slope_y) + viscosity * lap(v)) * w[0], 1)
                warm = (carried(temp) + diffusion * lap(temp) + heating) * w[0]
                put(new, cp, q, warm, 2)
                put(new, cp, q, (carried(salt) + diffusion * lap(salt)) * w[0], 3)
                growth0[cp, q] = reaction * jnp.exp(warming * warm) * w[0]

    def carry(old, cp, q, t, weight):
        c, x, z, n, s = around(old, cp, q, t)
        return weight[0] * c + weight[1] * x + weight[2] * z + weight[3] * n + weight[4] * s

    def substep(old, first, last, finish):
        for cp in range(first, last):
            for q in range(nrt):
                p = carry(old, cp, q, 0, [weights[cp, q, k] for k in range(5)])
                flat[line(cp, q), :] = water_extinction + pigment_extinction * p
        span = pl.ds(first * nrt * ROWS8, (last - first) * nrt * ROWS8)
        extinct = flat[span, :]
        irradiance = jnp.exp(-(running_sums(extinct) - 0.5 * extinct))
        flat[span, :] = irradiance / (irradiance + light_half)
        for cp in range(first, last):
            for q in range(nrt):
                growth[cp, q] = flat[line(cp, q), :] * growth0[cp, q]

        blank = jnp.zeros((ROWS8, LANES), F32)

        @pl.loop(first, last)
        def _(cp):
            def begin(q):
                weight = [weights[cp, q, k] for k in range(5)]
                advected, parts = [], []
                for t in range(ntr):
                    a = carry(old, cp, q, t, weight)
                    advected.append(a)
                    parts.append(a / (saturation + jnp.abs(a)))
                s = jnp.concatenate(parts + [blank], axis=0)
                high = s.astype(BF16)
                low = (s - high.astype(F32)).astype(BF16)
                return advected, jnp.concatenate([high, low, high], axis=0)

            def end(group, begun):
                parts = [b[1] for b in begun]
                s = parts[0] if len(parts) == 1 else jnp.concatenate(parts, axis=1)
                mixed = jnp.dot(mix_all, s, preferred_element_type=F32)
                for k, q in enumerate(group):
                    g = growth[cp, q]
                    for t in range(ntr):
                        block = mixed[t * ROWS8:(t + 1) * ROWS8, k * LANES:(k + 1) * LANES]
                        finish(cp, q, t, begun[k][0][t] + g * block)

            for q in range(0, nrt, 2):
                group = list(range(q, min(q + 2, nrt)))
                end(group, [begin(r) for r in group])

    def finish_in(ref):
        def finish(cp, q, t, value):
            put(ref, cp, q, value, t)

        return finish

    def finish_out(cp, q, t, value):
        start = q * (ntr * inner) + t * inner + (cp - halo // 2)
        result[pl.ds(start, ROWS8, stride=nrt * ntr * inner), :] = value

    edge = halo // 2
    ocean_step(ocean_a, ocean_b, stock_a)
    substep(stock_a, 0, ncp, finish_in(stock_b))
    substep(stock_b, edge // 2, ncp - edge // 2, finish_in(stock_a))
    ocean_step(ocean_b, ocean_a, stock_a)
    substep(stock_a, edge // 2, ncp - edge // 2, finish_in(stock_b))
    substep(stock_b, edge, ncp - edge, finish_out)
    send = pltpu.make_async_copy(result.at[pl.ds(halo * ntr * inner, rows * ntr * inner)], out, sem.at[0])
    send.start()
    for f in range(4):
        for cp in range(inner):
            for q in range(nrt):
                sea[f, cp, pl.ds(q, ROWS8, stride=nrt), :] = ocean_a[cp + edge, q + 1, f]
            ocean_out[f, :, pl.ds(cp * LANES, LANES)] = sea[f, cp, pl.ds(halo, rows), :]
    send.wait()


def run_window(tile, south, north, west, ocean, east, interaction, ntr, ncp):
    rows = ocean.shape[1]
    halo = HALO
    nrt = (rows + 2 * halo) // ROWS8
    inner = ncp - halo
    anywhere = pl.BlockSpec(memory_space=pl.ANY)
    inside = pl.BlockSpec(memory_space=pltpu.VMEM)
    return pl.pallas_call(
        main_kernel,
        out_shape=(
            jax.ShapeDtypeStruct((4, rows, inner * LANES), F32),
            jax.ShapeDtypeStruct((rows * ntr * inner, LANES), F32),
        ),
        in_specs=[anywhere] * 3 + [inside] * 4,
        out_specs=(inside, anywhere),
        scratch_shapes=[
            pltpu.VMEM(((rows + 2 * halo) * (ntr + 1) * ncp, LANES), F32),
            pltpu.VMEM((ncp, nrt + 2, ntr, ROWS8, LANES), F32),
            pltpu.VMEM((ncp, nrt + 2, ntr, ROWS8, LANES), F32),
            pltpu.VMEM((4, ncp, rows + 2 * halo, LANES), F32),
            pltpu.VMEM((2, halo * 4 * ncp, LANES), F32),
            pltpu.VMEM((ncp, nrt + 2, 4, ROWS8, LANES), F32),
            pltpu.VMEM((ncp, nrt + 2, 4, ROWS8, LANES), F32),
            pltpu.VMEM((ncp, nrt + 2, ROWS8, LANES), F32),
            pltpu.VMEM((ncp, nrt + 2, ROWS8, LANES), F32),
            pltpu.VMEM((ncp, nrt, 5, ROWS8, LANES), F32),
            pltpu.VMEM((ncp, nrt, ROWS8, LANES), F32),
            pltpu.VMEM((ncp, nrt, ROWS8, LANES), F32),
            pltpu.VMEM((ncp * nrt * ROWS8, LANES), F32),
            pltpu.VMEM(((rows + 2 * halo) * ntr * inner, LANES), F32),
            pltpu.SemaphoreType.DMA((1 + 4 * halo,)),
        ],
        compiler_params=pltpu.CompilerParams(vmem_limit_bytes=40 * 2**20),
        name="window",
    )(tile, south, north, west, ocean, east, interaction)


def shift(array, axis, by):
    count = lax.axis_size(axis)
    if by > 0:
        return lax.ppermute(array, axis, [(i, i + 1) for i in range(count - 1)])
    return lax.ppermute(array, axis, [(i + 1, i) for i in range(count - 1)])


def shards(ocean_fields, tracers, wet_levels, interaction):
    tiles = lax.axis_size("gx")
    ntr = tracers.shape[0]
    rows = ocean_fields.shape[1]
    columns = wet_levels.shape[1]
    levels = tracers.shape[2] // columns
    lines = tracers.shape[2] // LANES
    pair = LANES // levels
    inner = lines // tiles
    edge = HALO // pair
    ncp = inner + 2 * edge
    planes = ntr + 1

    margin = edge * LANES
    from_west = shift(ocean_fields[:, :, -margin:], "gx", 1)
    from_east = shift(ocean_fields[:, :, :margin], "gx", -1)
    depth = jnp.broadcast_to(wet_levels.astype(F32).reshape(lines, pair, 1), (lines, pair, levels))
    sent = cut_windows(tracers.reshape(ntr, lines, 1, LANES), depth.reshape(1, lines, 1, LANES), tiles, ncp)
    tile = lax.all_to_all(sent.reshape(tiles, planes * ncp, LANES), "gx", split_axis=0, concat_axis=0, tiled=True)
    to_north, to_south = row_messages(tile, from_west, ocean_fields, from_east, ncp)
    south = shift(to_north, "grp", 1)
    north = shift(to_south, "grp", -1)
    ocean_next, result = run_window(
        tile.reshape(-1, LANES), south, north, from_west, ocean_fields, from_east, interaction, ntr, ncp
    )
    back = lax.all_to_all(result.reshape(tiles, ntr * inner, LANES), "gx", split_axis=0, concat_axis=0, tiled=True)
    back = back.reshape(tiles, ntr, inner, LANES).transpose(1, 0, 2, 3)
    return ocean_next, back.reshape(ntr, 1, lines * LANES)


def solution(mesh):
    placed = (P(None, "grp", "gx"), P(None, ("grp", "gx"), None), P(("grp", "gx"), None), P())
    return jax.shard_map(
        shards,
        mesh=mesh,
        in_specs=placed,
        out_specs=(P(None, "grp", "gx"), P(None, ("grp", "gx"), None)),
        check_vma=False,
    )
```

```python
import jax
import jax.numpy as jnp
from jax import lax
from jax.experimental import pallas as pl
from jax.experimental.pallas import tpu as pltpu
from jax.sharding import PartitionSpec as P

NC = 2
NB = 2
HALO = NC * NB

courant = 0.2
diffusion = 0.08
viscosity = 0.08
time_step = 0.1
thermal = 0.2
haline = 0.15
gravity = 0.1
coriolis = 0.5
coriolis_slope = 0.5
water_extinction = 0.04
pigment_extinction = 0.01
heating_rate = 0.5
light_half = 0.3
warming = 0.1
saturation = 0.5
reaction = 0.5

LANES = 128
ROWS8 = 8
F32 = jnp.float32
BF16 = jnp.bfloat16


def window_kernel(strip, depth_plane, out, big, sem_in, sem_out):
    planes, lines = big.shape[0], strip.shape[1]
    tiles, wide = out.shape[0], out.shape[2]
    step = lines // tiles
    edge = (wide - step) // 2
    tracers_in = pltpu.make_async_copy(strip, big.at[pl.ds(0, planes - 1), pl.ds(edge, lines)], sem_in.at[0])
    depth_in = pltpu.make_async_copy(depth_plane, big.at[pl.ds(planes - 1, 1), pl.ds(edge, lines)], sem_in.at[1])
    tracers_in.start()
    depth_in.start()
    zeros = jnp.zeros((planes, edge, 1, LANES), F32)
    big[:, pl.ds(0, edge)] = zeros
    big[:, pl.ds(edge + lines, edge)] = zeros
    tracers_in.wait()
    depth_in.wait()

    def send(d):
        return pltpu.make_async_copy(big.at[:, pl.ds(d * step, wide)], out.at[d], sem_out.at[d])

    @pl.loop(0, tiles)
    def _(d):
        send(d).start()

    @pl.loop(0, tiles)
    def _(d):
        send(d).wait()


def cut_windows(strip, depth_plane, tiles, wide):
    planes = strip.shape[0] + 1
    lines = strip.shape[1]
    edge = (wide - lines // tiles) // 2
    anywhere = pl.BlockSpec(memory_space=pl.ANY)
    return pl.pallas_call(
        window_kernel,
        out_shape=jax.ShapeDtypeStruct((tiles, planes, wide, 1, LANES), F32),
        in_specs=[anywhere, anywhere],
        out_specs=anywhere,
        scratch_shapes=[
            pltpu.VMEM((planes, lines + 2 * edge, 1, LANES), F32),
            pltpu.SemaphoreType.DMA((2,)),
            pltpu.SemaphoreType.DMA((tiles,)),
        ],
        name="cut_windows",
    )(strip, depth_plane)


def edge_kernel(tile, west, ocean, east, to_north, to_south, lines, sem):
    planes_lines = tile.shape[1]
    rows = ocean.shape[1]
    halo = HALO
    wide = lines.shape[1] // halo
    sides = ((to_north, rows - halo), (to_south, 0))
    copies = [
        pltpu.make_async_copy(
            tile.at[first + r],
            message.at[pl.ds(r * (planes_lines + wide), planes_lines)],
            sem.at[k * halo + r],
        )
        for k, (message, first) in enumerate(sides)
        for r in range(halo)
    ]
    for copy in copies:
        copy.start()
    for k, (message, first) in enumerate(sides):
        c = 0
        for f in range(4):
            for part in (west, ocean, east):
                for j in range(part.shape[2] // LANES):
                    lines[k, pl.ds(c, halo, stride=wide), :] = part[f, pl.ds(first, halo), pl.ds(j * LANES, LANES)]
                    c += 1
    more = [
        pltpu.make_async_copy(
            lines.at[k, pl.ds(r * wide, wide)],
            message.at[pl.ds(r * (planes_lines + wide) + planes_lines, wide)],
            sem.at[(2 + k) * halo + r],
        )
        for k, (message, first) in enumerate(sides)
        for r in range(halo)
    ]
    for copy in more:
        copy.start()
    for copy in copies + more:
        copy.wait()


def row_messages(tile, west, ocean, east, ncp):
    anywhere = pl.BlockSpec(memory_space=pl.ANY)
    inside = pl.BlockSpec(memory_space=pltpu.VMEM)
    message = jax.ShapeDtypeStruct((HALO * (tile.shape[1] + 4 * ncp), LANES), F32)
    return pl.pallas_call(
        edge_kernel,
        out_shape=(message, message),
        in_specs=[anywhere, inside, inside, inside],
        out_specs=(anywhere, anywhere),
        scratch_shapes=[
            pltpu.VMEM((2, HALO * 4 * ncp, LANES), F32),
            pltpu.SemaphoreType.DMA((4 * HALO,)),
        ],
        compiler_params=pltpu.CompilerParams(vmem_limit_bytes=8 * 2**20),
        name="row_messages",
    )(tile, west, ocean, east)


def main_kernel(
    tile, south, north, west, ocean, east, mix_ref, ocean_out, out,
    raw, stock_a, stock_b, sea, beyond, ocean_a, ocean_b, press, wet, weights, growth0, growth, flat, held_a, held_b, result, sem,
):
    ncp, nrt, ntr = stock_a.shape[0], stock_a.shape[1] - 2, stock_a.shape[2]
    planes = ntr + 1
    line_stride = planes * ncp
    rows = tile.shape[0] // line_stride
    halo = HALO
    inner = ncp - halo
    wide_ocean = 4 * ncp
    copies = [
        pltpu.make_async_copy(tile, raw.at[pl.ds(halo * line_stride, rows * line_stride)], sem.at[0]),
    ]
    for side, message in enumerate((south, north)):
        for r in range(halo):
            start = r * (line_stride + wide_ocean)
            row = r + side * (halo + rows)
            copies.append(pltpu.make_async_copy(
                message.at[pl.ds(start, line_stride)], raw.at[pl.ds(row * line_stride, line_stride)],
                sem.at[len(copies)],
            ))
            copies.append(pltpu.make_async_copy(
                message.at[pl.ds(start + line_stride, wide_ocean)], beyond.at[side, pl.ds(r * wide_ocean, wide_ocean)],
                sem.at[len(copies)],
            ))
    for copy in copies:
        copy.start()

    lane = lax.broadcasted_iota(jnp.int32, (ROWS8, LANES), 1)
    sub = lax.broadcasted_iota(jnp.int32, (ROWS8, LANES), 0)
    half = LANES // 2
    left = lane < half
    level_f = (lane % half).astype(F32)

    def swap(x):
        return pltpu.roll(x, half, 1)

    def put(ref, cp, q, value, *more):
        ref[(cp, q + 1, *more)] = value
        if q == 0:
            ref[(cp, nrt + 1, *more)] = pltpu.roll(value, ROWS8 - 1, 0)
        if q == nrt - 1:
            ref[(cp, 0, *more)] = pltpu.roll(value, 1, 0)

    def around(ref, cp, q, *more):
        right = ref[(jnp.minimum(cp + 1, ncp - 1), q + 1, *more)]
        leftward = ref[(jnp.maximum(cp - 1, 0), q + 1, *more)]
        centre = ref[(cp, q + 1, *more)]
        far = swap(jnp.where(left, right, leftward))
        return centre, swap(centre), far, ref[(cp, q + 2, *more)], ref[(cp, q, *more)]

    def five(ref, cp, q, *more):
        centre, swapped, far, cell_north, cell_south = around(ref, cp, q, *more)
        return centre, jnp.where(left, swapped, far), jnp.where(left, far, swapped), cell_north, cell_south

    row_id = lax.broadcasted_iota(jnp.int32, (LANES, LANES), 0)
    col_id = lax.broadcasted_iota(jnp.int32, (LANES, LANES), 1)
    upper = ((row_id <= col_id) & (row_id // half == col_id // half)).astype(F32).astype(BF16)

    def running_sums(x):
        high = x.astype(BF16)
        rest = x - high.astype(F32)
        middle = rest.astype(BF16)
        low = (rest - middle.astype(F32)).astype(BF16)
        return (
            jnp.dot(high, upper, preferred_element_type=F32)
            + jnp.dot(middle, upper, preferred_element_type=F32)
            + jnp.dot(low, upper, preferred_element_type=F32)
        )

    wide = ntr * ROWS8
    deep = (ntr + 1) * ROWS8
    pick = (lax.broadcasted_iota(jnp.int32, (wide, ntr), 0) // ROWS8 == lax.broadcasted_iota(jnp.int32, (wide, ntr), 1)).astype(F32).astype(BF16)
    pick_t = (lax.broadcasted_iota(jnp.int32, (ntr, deep), 1) // ROWS8 == lax.broadcasted_iota(jnp.int32, (ntr, deep), 0)).astype(F32).astype(BF16)
    same = lax.broadcasted_iota(jnp.int32, (wide, deep), 0) % ROWS8 == lax.broadcasted_iota(jnp.int32, (wide, deep), 1) % ROWS8

    def spread(part):
        tall = jnp.dot(pick, part, preferred_element_type=F32).astype(BF16)
        return jnp.where(same, jnp.dot(tall, pick_t, preferred_element_type=F32), 0.0)

    mix = mix_ref[...]
    mix_hi = mix.astype(BF16)
    mix_lo = (mix - mix_hi.astype(F32)).astype(BF16)
    spread_hi = spread(mix_hi)
    mix_all = jnp.concatenate([spread_hi, spread_hi, spread(mix_lo)], axis=1).astype(BF16)

    for copy in copies:
        copy.wait()

    for f in range(4):
        for cp in range(ncp):
            if cp < halo // 2:
                part, j = west, cp
            elif cp < ncp - halo // 2:
                part, j = ocean, cp - halo // 2
            else:
                part, j = east, cp - (ncp - halo // 2)
            sea[f, cp, pl.ds(0, halo), :] = beyond[0, pl.ds(f * ncp + cp, halo, stride=wide_ocean), :]
            sea[f, cp, pl.ds(halo, rows), :] = part[f, :, pl.ds(j * LANES, LANES)]
            sea[f, cp, pl.ds(halo + rows, halo), :] = beyond[1, pl.ds(f * ncp + cp, halo, stride=wide_ocean), :]
            for q in range(nrt):
                put(ocean_a, cp, q, sea[f, cp, pl.ds(q, ROWS8, stride=nrt), :], f)

    @pl.loop(0, ncp)
    def _(cp):
        for q in range(nrt):
            base = q * line_stride + cp
            for t in range(ntr):
                put(stock_a, cp, q, raw[pl.ds(base + t * ncp, ROWS8, stride=nrt * line_stride), :], t)
            depth = raw[pl.ds(base + ntr * ncp, ROWS8, stride=nrt * line_stride), :]
            put(wet, cp, q, (level_f < depth).astype(F32))

    first_row = lax.axis_index("grp") * rows - halo
    total_rows = rows * lax.axis_size("grp")

    def line(cp, q):
        return pl.ds((cp * nrt + q) * ROWS8, ROWS8)

    def ocean_step(old, new, stock):
        for cp in range(ncp):
            for q in range(nrt):
                flat[line(cp, q), :] = (haline * old[cp, q + 1, 3] - thermal * old[cp, q + 1, 2]) * wet[cp, q + 1]
        flat[...] = gravity * running_sums(flat[...])
        for cp in range(ncp):
            for q in range(nrt):
                put(press, cp, q, flat[line(cp, q), :])
        for cp in range(ncp):
            for q in range(nrt):
                flat[line(cp, q), :] = water_extinction + pigment_extinction * stock[cp, q + 1, 0]
        extinct_all = flat[...]
        flat[...] = heating_rate * extinct_all * jnp.exp(-(running_sums(extinct_all) - 0.5 * extinct_all))

        @pl.loop(0, ncp)
        def _(cp):
            for q in range(nrt):
                w = five(wet, cp, q)
                open_e, open_w, open_n, open_s = (w[0] * w[k] for k in range(1, 5))
                u = five(old, cp, q, 0)
                v = five(old, cp, q, 1)
                temp = five(old, cp, q, 2)
                salt = five(old, cp, q, 3)
                p = five(press, cp, q)
                fe = 0.5 * (u[0] + u[1]) * open_e
                fw = 0.5 * (u[0] + u[2]) * open_w
                fn = 0.5 * (v[0] + v[3]) * open_n
                fs = 0.5 * (v[0] + v[4]) * open_s
                slope_x = 0.5 * (open_e * (p[1] - p[0]) + open_w * (p[0] - p[2]))
                slope_y = 0.5 * (open_n * (p[3] - p[0]) + open_s * (p[0] - p[4]))
                row = (first_row + q + nrt * sub).astype(F32)
                f = coriolis + coriolis_slope * ((row + 0.5) / total_rows - 0.5)
                heating = flat[pl.ds(pl.multiple_of((cp * nrt + q) * ROWS8, ROWS8), ROWS8), :]

                def lap(x):
                    return open_e * (x[1] - x[0]) + open_w * (x[2] - x[0]) + open_n * (x[3] - x[0]) + open_s * (x[4] - x[0])

                we = -courant * jnp.minimum(fe, 0.0)
                ww = courant * jnp.maximum(fw, 0.0)
                wn = -courant * jnp.minimum(fn, 0.0)
                ws = courant * jnp.maximum(fs, 0.0)
                wc = 1.0 - courant * (
                    jnp.maximum(fe, 0.0) - jnp.minimum(fw, 0.0) + jnp.maximum(fn, 0.0) - jnp.minimum(fs, 0.0)
                )

                def carried(x):
                    return wc * x[0] + we * x[1] + ww * x[2] + wn * x[3] + ws * x[4]

                weights[cp, q, 0] = wc
                weights[cp, q, 1] = jnp.where(left, we, ww)
                weights[cp, q, 2] = jnp.where(left, ww, we)
                weights[cp, q, 3] = wn
                weights[cp, q, 4] = ws
                put(new, cp, q, (u[0] + time_step * (f * v[0] - slope_x) + viscosity * lap(u)) * w[0], 0)
                put(new, cp, q, (v[0] + time_step * (-f * u[0] - slope_y) + viscosity * lap(v)) * w[0], 1)
                warm = (carried(temp) + diffusion * lap(temp) + heating) * w[0]
                put(new, cp, q, warm, 2)
                put(new, cp, q, (carried(salt) + diffusion * lap(salt)) * w[0], 3)
                growth0[cp, q] = reaction * jnp.exp(warming * warm) * w[0]

    def carry(old, cp, q, t, weight):
        c, x, z, n, s = around(old, cp, q, t)
        return weight[0] * c + weight[1] * x + weight[2] * z + weight[3] * n + weight[4] * s

    def substep(old, new, first, last, finish):
        for cp in range(first, last):
            for q in range(nrt):
                p = carry(old, cp, q, 0, [weights[cp, q, k] for k in range(5)])
                flat[line(cp, q), :] = water_extinction + pigment_extinction * p
        span = pl.ds(first * nrt * ROWS8, (last - first) * nrt * ROWS8)
        extinct = flat[span, :]
        irradiance = jnp.exp(-(running_sums(extinct) - 0.5 * extinct))
        flat[span, :] = irradiance / (irradiance + light_half)
        for cp in range(first, last):
            for q in range(nrt):
                growth[cp, q] = flat[line(cp, q), :] * growth0[cp, q]

        blank = jnp.zeros((ROWS8, LANES), F32)

        def begin(cp, held):
            for q in range(nrt):
                weight = [weights[cp, q, k] for k in range(5)]
                parts = []
                for t in range(ntr):
                    a = carry(old, cp, q, t, weight)
                    new[cp, q + 1, t] = a
                    parts.append(a / (saturation + jnp.abs(a)))
                s = jnp.concatenate(parts + [blank], axis=0)
                high = s.astype(BF16)
                held[pl.ds(0, deep), pl.ds(q * LANES, LANES)] = high
                held[pl.ds(deep, deep), pl.ds(q * LANES, LANES)] = (s - high.astype(F32)).astype(BF16)

        def end(cp, held):
            for q in range(0, nrt, 2):
                group = range(q, min(q + 2, nrt))
                across = pl.ds(q * LANES, len(group) * LANES)
                high = held[pl.ds(0, deep), across]
                s = jnp.concatenate([high, held[pl.ds(deep, deep), across], high], axis=0)
                mixed = jnp.dot(mix_all, s, preferred_element_type=F32)
                for k, r in enumerate(group):
                    g = growth[cp, r]
                    for t in range(ntr):
                        block = mixed[t * ROWS8:(t + 1) * ROWS8, k * LANES:(k + 1) * LANES]
                        finish(cp, r, t, new[cp, r + 1, t] + g * block)

        begin(first, held_a)

        @pl.loop(0, (last - first) // 2 - 1)
        def _(k):
            cp = first + 2 * k
            begin(cp + 1, held_b)
            end(cp, held_a)
            begin(cp + 2, held_a)
            end(cp + 1, held_b)

        begin(last - 1, held_b)
        end(last - 2, held_a)
        end(last - 1, held_b)

    def finish_in(ref):
        def finish(cp, q, t, value):
            put(ref, cp, q, value, t)

        return finish

    def finish_out(cp, q, t, value):
        start = q * (ntr * inner) + t * inner + (cp - halo // 2)
        result[pl.ds(start, ROWS8, stride=nrt * ntr * inner), :] = value

    edge = halo // 2
    ocean_step(ocean_a, ocean_b, stock_a)
    substep(stock_a, stock_b, 0, ncp, finish_in(stock_b))
    substep(stock_b, stock_a, edge // 2, ncp - edge // 2, finish_in(stock_a))
    ocean_step(ocean_b, ocean_a, stock_a)
    substep(stock_a, stock_b, edge // 2, ncp - edge // 2, finish_in(stock_b))
    substep(stock_b, stock_a, edge, ncp - edge, finish_out)
    send = pltpu.make_async_copy(result.at[pl.ds(halo * ntr * inner, rows * ntr * inner)], out, sem.at[0])
    send.start()
    for f in range(4):
        for cp in range(inner):
            for q in range(nrt):
                sea[f, cp, pl.ds(q, ROWS8, stride=nrt), :] = ocean_a[cp + edge, q + 1, f]
            ocean_out[f, :, pl.ds(cp * LANES, LANES)] = sea[f, cp, pl.ds(halo, rows), :]
    send.wait()


def run_window(tile, south, north, west, ocean, east, interaction, ntr, ncp):
    rows = ocean.shape[1]
    halo = HALO
    nrt = (rows + 2 * halo) // ROWS8
    inner = ncp - halo
    anywhere = pl.BlockSpec(memory_space=pl.ANY)
    inside = pl.BlockSpec(memory_space=pltpu.VMEM)
    return pl.pallas_call(
        main_kernel,
        out_shape=(
            jax.ShapeDtypeStruct((4, rows, inner * LANES), F32),
            jax.ShapeDtypeStruct((rows * ntr * inner, LANES), F32),
        ),
        in_specs=[anywhere] * 3 + [inside] * 4,
        out_specs=(inside, anywhere),
        scratch_shapes=[
            pltpu.VMEM(((rows + 2 * halo) * (ntr + 1) * ncp, LANES), F32),
            pltpu.VMEM((ncp, nrt + 2, ntr, ROWS8, LANES), F32),
            pltpu.VMEM((ncp, nrt + 2, ntr, ROWS8, LANES), F32),
            pltpu.VMEM((4, ncp, rows + 2 * halo, LANES), F32),
            pltpu.VMEM((2, halo * 4 * ncp, LANES), F32),
            pltpu.VMEM((ncp, nrt + 2, 4, ROWS8, LANES), F32),
            pltpu.VMEM((ncp, nrt + 2, 4, ROWS8, LANES), F32),
            pltpu.VMEM((ncp, nrt + 2, ROWS8, LANES), F32),
            pltpu.VMEM((ncp, nrt + 2, ROWS8, LANES), F32),
            pltpu.VMEM((ncp, nrt, 5, ROWS8, LANES), F32),
            pltpu.VMEM((ncp, nrt, ROWS8, LANES), F32),
            pltpu.VMEM((ncp, nrt, ROWS8, LANES), F32),
            pltpu.VMEM((ncp * nrt * ROWS8, LANES), F32),
            pltpu.VMEM((2 * (ntr + 1) * ROWS8, nrt * LANES), BF16),
            pltpu.VMEM((2 * (ntr + 1) * ROWS8, nrt * LANES), BF16),
            pltpu.VMEM(((rows + 2 * halo) * ntr * inner, LANES), F32),
            pltpu.SemaphoreType.DMA((1 + 4 * halo,)),
        ],
        compiler_params=pltpu.CompilerParams(vmem_limit_bytes=40 * 2**20),
        name="window",
    )(tile, south, north, west, ocean, east, interaction)


def shift(array, axis, by):
    count = lax.axis_size(axis)
    if by > 0:
        return lax.ppermute(array, axis, [(i, i + 1) for i in range(count - 1)])
    return lax.ppermute(array, axis, [(i + 1, i) for i in range(count - 1)])


def shards(ocean_fields, tracers, wet_levels, interaction):
    tiles = lax.axis_size("gx")
    ntr = tracers.shape[0]
    rows = ocean_fields.shape[1]
    columns = wet_levels.shape[1]
    levels = tracers.shape[2] // columns
    lines = tracers.shape[2] // LANES
    pair = LANES // levels
    inner = lines // tiles
    edge = HALO // pair
    ncp = inner + 2 * edge
    planes = ntr + 1

    margin = edge * LANES
    from_west = shift(ocean_fields[:, :, -margin:], "gx", 1)
    from_east = shift(ocean_fields[:, :, :margin], "gx", -1)
    depth = jnp.broadcast_to(wet_levels.astype(F32).reshape(lines, pair, 1), (lines, pair, levels))
    sent = cut_windows(tracers.reshape(ntr, lines, 1, LANES), depth.reshape(1, lines, 1, LANES), tiles, ncp)
    tile = lax.all_to_all(sent.reshape(tiles, planes * ncp, LANES), "gx", split_axis=0, concat_axis=0, tiled=True)
    to_north, to_south = row_messages(tile, from_west, ocean_fields, from_east, ncp)
    south = shift(to_north, "grp", 1)
    north = shift(to_south, "grp", -1)
    ocean_next, result = run_window(
        tile.reshape(-1, LANES), south, north, from_west, ocean_fields, from_east, interaction, ntr, ncp
    )
    back = lax.all_to_all(result.reshape(tiles, ntr * inner, LANES), "gx", split_axis=0, concat_axis=0, tiled=True)
    back = back.reshape(tiles, ntr, inner, LANES).transpose(1, 0, 2, 3)
    return ocean_next, back.reshape(ntr, 1, lines * LANES)


def solution(mesh):
    placed = (P(None, "grp", "gx"), P(None, ("grp", "gx"), None), P(("grp", "gx"), None), P())
    return jax.shard_map(
        shards,
        mesh=mesh,
        in_specs=placed,
        out_specs=(P(None, "grp", "gx"), P(None, ("grp", "gx"), None)),
        check_vma=False,
    )
```

```python
import jax
import jax.numpy as jnp
from jax import lax
from jax.experimental import pallas as pl
from jax.experimental.pallas import tpu as pltpu
from jax.sharding import PartitionSpec as P

NC = 2
NB = 2
HALO = NC * NB

courant = 0.2
diffusion = 0.08
viscosity = 0.08
time_step = 0.1
thermal = 0.2
haline = 0.15
gravity = 0.1
coriolis = 0.5
coriolis_slope = 0.5
water_extinction = 0.04
pigment_extinction = 0.01
heating_rate = 0.5
light_half = 0.3
warming = 0.1
saturation = 0.5
reaction = 0.5

LANES = 128
ROWS8 = 8
F32 = jnp.float32
BF16 = jnp.bfloat16


GROUP = 4
PIECES = 4


def window_kernel(strip, depth_lines, out, big, depth, sem_in, sem_out):
    ntr, lines = strip.shape[0], strip.shape[1]
    tiles, groups = out.shape[0], (out.shape[1] - 1) // ntr
    step = lines // tiles
    edge = (big.shape[1] - lines) // 2
    span = lines // PIECES
    arrivals = [
        pltpu.make_async_copy(strip.at[:, pl.ds(p * span, span)], big.at[:, pl.ds(edge + p * span, span)], sem_in.at[p])
        for p in range(PIECES)
    ]
    depth_in = pltpu.make_async_copy(depth_lines, depth, sem_in.at[PIECES])
    for copy in [depth_in] + arrivals:
        copy.start()
    zeros = jnp.zeros((ntr, edge, 1, LANES), F32)
    big[:, pl.ds(0, edge)] = zeros
    big[:, pl.ds(edge + lines, edge)] = zeros

    def sends(d):
        window = [
            pltpu.make_async_copy(
                big.at[:, pl.ds(d * step + g * GROUP, GROUP)], out.at[d, pl.ds(g * ntr, ntr)], sem_out.at[d, g]
            )
            for g in range(groups)
        ]
        return window + [pltpu.make_async_copy(depth.at[d], out.at[d, groups * ntr], sem_out.at[d, groups])]

    depth_in.wait()
    first = 0
    for p in range(PIECES):
        arrivals[p].wait()
        last = tiles if p == PIECES - 1 else (span * (p + 1) + edge - groups * GROUP) // step + 1

        @pl.loop(first, last)
        def _(d):
            for copy in sends(d):
                copy.start()

        first = last

    @pl.loop(0, tiles)
    def _(d):
        for copy in sends(d):
            copy.wait()


def cut_windows(strip, depth_lines, tiles, wide):
    ntr, lines = strip.shape[0], strip.shape[1]
    groups = wide // GROUP
    edge = (wide - lines // tiles) // 2
    anywhere = pl.BlockSpec(memory_space=pl.ANY)
    return pl.pallas_call(
        window_kernel,
        out_shape=jax.ShapeDtypeStruct((tiles, groups * ntr + 1, GROUP, 1, LANES), F32),
        in_specs=[anywhere, anywhere],
        out_specs=anywhere,
        scratch_shapes=[
            pltpu.VMEM((ntr, lines + 2 * edge, 1, LANES), F32),
            pltpu.VMEM((tiles, GROUP, 1, LANES), F32),
            pltpu.SemaphoreType.DMA((PIECES + 1,)),
            pltpu.SemaphoreType.DMA((tiles, groups + 1)),
        ],
        name="cut_windows",
    )(strip, depth_lines)


def edge_kernel(tile, west, ocean, east, to_north, to_south, lines, sem):
    rows = ocean.shape[1]
    halo = HALO
    wide = lines.shape[1] // halo
    per_row = tile.shape[0] // rows
    sides = ((to_north, rows - halo), (to_south, 0))
    copies = [
        pltpu.make_async_copy(
            tile.at[pl.ds(first * per_row, halo * per_row)], message.at[pl.ds(0, halo * per_row)], sem.at[k]
        )
        for k, (message, first) in enumerate(sides)
    ]
    for copy in copies:
        copy.start()
    for k, (message, first) in enumerate(sides):
        c = 0
        for f in range(4):
            for part in (west, ocean, east):
                for j in range(part.shape[2] // LANES):
                    lines[k, pl.ds(c, halo, stride=wide), :] = part[f, pl.ds(first, halo), pl.ds(j * LANES, LANES)]
                    c += 1
    more = [
        pltpu.make_async_copy(lines.at[k], message.at[pl.ds(halo * per_row, halo * wide)], sem.at[2 + k])
        for k, (message, first) in enumerate(sides)
    ]
    for copy in more:
        copy.start()
    for copy in copies + more:
        copy.wait()


def row_messages(tile, west, ocean, east, ncp):
    anywhere = pl.BlockSpec(memory_space=pl.ANY)
    inside = pl.BlockSpec(memory_space=pltpu.VMEM)
    message = jax.ShapeDtypeStruct((HALO * (tile.shape[0] // ocean.shape[1] + 4 * ncp), LANES), F32)
    return pl.pallas_call(
        edge_kernel,
        out_shape=(message, message),
        in_specs=[anywhere, inside, inside, inside],
        out_specs=(anywhere, anywhere),
        scratch_shapes=[
            pltpu.VMEM((2, HALO * 4 * ncp, LANES), F32),
            pltpu.SemaphoreType.DMA((4,)),
        ],
        compiler_params=pltpu.CompilerParams(vmem_limit_bytes=8 * 2**20),
        name="row_messages",
    )(tile, west, ocean, east)


def main_kernel(
    tile, south, north, west, ocean, east, mix_ref, ocean_out, out,
    raw, stock_a, stock_b, sea, beyond, ocean_a, ocean_b, press, wet, weights, growth0, growth, flat, held_a, held_b, result, sem,
):
    ncp, nrt, ntr = stock_a.shape[0], stock_a.shape[1] - 2, stock_a.shape[2]
    rows = ocean.shape[1]
    line_stride = tile.shape[0] // rows
    groups = ncp // GROUP
    halo = HALO
    inner = ncp - halo
    wide_ocean = 4 * ncp
    many = halo * line_stride
    copies = [
        pltpu.make_async_copy(tile, raw.at[pl.ds(many, rows * line_stride)], sem.at[0]),
        pltpu.make_async_copy(south.at[pl.ds(0, many)], raw.at[pl.ds(0, many)], sem.at[1]),
        pltpu.make_async_copy(north.at[pl.ds(0, many)], raw.at[pl.ds((halo + rows) * line_stride, many)], sem.at[2]),
        pltpu.make_async_copy(south.at[pl.ds(many, halo * wide_ocean)], beyond.at[0], sem.at[3]),
        pltpu.make_async_copy(north.at[pl.ds(many, halo * wide_ocean)], beyond.at[1], sem.at[4]),
    ]
    for copy in copies:
        copy.start()

    lane = lax.broadcasted_iota(jnp.int32, (ROWS8, LANES), 1)
    sub = lax.broadcasted_iota(jnp.int32, (ROWS8, LANES), 0)
    half = LANES // 2
    left = lane < half
    level_f = (lane % half).astype(F32)

    def swap(x):
        return pltpu.roll(x, half, 1)

    def put(ref, cp, q, value, *more):
        ref[(cp, q + 1, *more)] = value
        if q == 0:
            ref[(cp, nrt + 1, *more)] = pltpu.roll(value, ROWS8 - 1, 0)
        if q == nrt - 1:
            ref[(cp, 0, *more)] = pltpu.roll(value, 1, 0)

    def around(ref, cp, q, *more):
        right = ref[(jnp.minimum(cp + 1, ncp - 1), q + 1, *more)]
        leftward = ref[(jnp.maximum(cp - 1, 0), q + 1, *more)]
        centre = ref[(cp, q + 1, *more)]
        far = swap(jnp.where(left, right, leftward))
        return centre, swap(centre), far, ref[(cp, q + 2, *more)], ref[(cp, q, *more)]

    def five(ref, cp, q, *more):
        centre, swapped, far, cell_north, cell_south = around(ref, cp, q, *more)
        return centre, jnp.where(left, swapped, far), jnp.where(left, far, swapped), cell_north, cell_south

    row_id = lax.broadcasted_iota(jnp.int32, (LANES, LANES), 0)
    col_id = lax.broadcasted_iota(jnp.int32, (LANES, LANES), 1)
    upper = ((row_id <= col_id) & (row_id // half == col_id // half)).astype(F32).astype(BF16)

    def running_sums(x):
        high = x.astype(BF16)
        rest = x - high.astype(F32)
        middle = rest.astype(BF16)
        low = (rest - middle.astype(F32)).astype(BF16)
        return (
            jnp.dot(high, upper, preferred_element_type=F32)
            + jnp.dot(middle, upper, preferred_element_type=F32)
            + jnp.dot(low, upper, preferred_element_type=F32)
        )

    wide = ntr * ROWS8
    deep = (ntr + 1) * ROWS8
    pick = (lax.broadcasted_iota(jnp.int32, (wide, ntr), 0) // ROWS8 == lax.broadcasted_iota(jnp.int32, (wide, ntr), 1)).astype(F32).astype(BF16)
    pick_t = (lax.broadcasted_iota(jnp.int32, (ntr, deep), 1) // ROWS8 == lax.broadcasted_iota(jnp.int32, (ntr, deep), 0)).astype(F32).astype(BF16)
    same = lax.broadcasted_iota(jnp.int32, (wide, deep), 0) % ROWS8 == lax.broadcasted_iota(jnp.int32, (wide, deep), 1) % ROWS8

    def spread(part):
        tall = jnp.dot(pick, part, preferred_element_type=F32).astype(BF16)
        return jnp.where(same, jnp.dot(tall, pick_t, preferred_element_type=F32), 0.0)

    mix = mix_ref[...]
    mix_hi = mix.astype(BF16)
    mix_lo = (mix - mix_hi.astype(F32)).astype(BF16)
    spread_hi = spread(mix_hi)
    mix_all = jnp.concatenate([spread_hi, spread_hi, spread(mix_lo)], axis=1).astype(BF16)

    for copy in copies:
        copy.wait()

    for f in range(4):
        for cp in range(ncp):
            if cp < halo // 2:
                part, j = west, cp
            elif cp < ncp - halo // 2:
                part, j = ocean, cp - halo // 2
            else:
                part, j = east, cp - (ncp - halo // 2)
            sea[f, cp, pl.ds(0, halo), :] = beyond[0, pl.ds(f * ncp + cp, halo, stride=wide_ocean), :]
            sea[f, cp, pl.ds(halo, rows), :] = part[f, :, pl.ds(j * LANES, LANES)]
            sea[f, cp, pl.ds(halo + rows, halo), :] = beyond[1, pl.ds(f * ncp + cp, halo, stride=wide_ocean), :]
            for q in range(nrt):
                put(ocean_a, cp, q, sea[f, cp, pl.ds(q, ROWS8, stride=nrt), :], f)

    def spaced(start):
        return pl.ds(start, ROWS8, stride=nrt * line_stride)

    depths = jnp.concatenate(
        [raw[spaced(q * line_stride + groups * ntr * GROUP), :] for q in range(nrt)] + [jnp.zeros((ROWS8, LANES), F32)], axis=0
    ).astype(BF16)

    @pl.loop(0, ncp)
    def _(cp):
        of_pair = (row_id == 2 * cp + col_id // half).astype(F32).astype(BF16)
        depth = jnp.dot(depths, of_pair, preferred_element_type=F32)
        for q in range(nrt):
            base = q * line_stride + (cp // GROUP) * (ntr * GROUP) + cp % GROUP
            for t in range(ntr):
                put(stock_a, cp, q, raw[spaced(base + t * GROUP), :], t)
            put(wet, cp, q, (level_f < depth[q * ROWS8:(q + 1) * ROWS8]).astype(F32))

    first_row = lax.axis_index("grp") * rows - halo
    total_rows = rows * lax.axis_size("grp")

    def line(cp, q):
        return pl.ds((cp * nrt + q) * ROWS8, ROWS8)

    def ocean_step(old, new, stock):
        for cp in range(ncp):
            for q in range(nrt):
                flat[line(cp, q), :] = (haline * old[cp, q + 1, 3] - thermal * old[cp, q + 1, 2]) * wet[cp, q + 1]
        flat[...] = gravity * running_sums(flat[...])
        for cp in range(ncp):
            for q in range(nrt):
                put(press, cp, q, flat[line(cp, q), :])
        for cp in range(ncp):
            for q in range(nrt):
                flat[line(cp, q), :] = water_extinction + pigment_extinction * stock[cp, q + 1, 0]
        extinct_all = flat[...]
        flat[...] = heating_rate * extinct_all * jnp.exp(-(running_sums(extinct_all) - 0.5 * extinct_all))

        @pl.loop(0, ncp)
        def _(cp):
            for q in range(nrt):
                w = five(wet, cp, q)
                open_e, open_w, open_n, open_s = (w[0] * w[k] for k in range(1, 5))
                u = five(old, cp, q, 0)
                v = five(old, cp, q, 1)
                temp = five(old, cp, q, 2)
                salt = five(old, cp, q, 3)
                p = five(press, cp, q)
                fe = 0.5 * (u[0] + u[1]) * open_e
                fw = 0.5 * (u[0] + u[2]) * open_w
                fn = 0.5 * (v[0] + v[3]) * open_n
                fs = 0.5 * (v[0] + v[4]) * open_s
                slope_x = 0.5 * (open_e * (p[1] - p[0]) + open_w * (p[0] - p[2]))
                slope_y = 0.5 * (open_n * (p[3] - p[0]) + open_s * (p[0] - p[4]))
                row = (first_row + q + nrt * sub).astype(F32)
                f = coriolis + coriolis_slope * ((row + 0.5) / total_rows - 0.5)
                heating = flat[pl.ds(pl.multiple_of((cp * nrt + q) * ROWS8, ROWS8), ROWS8), :]

                def lap(x):
                    return open_e * (x[1] - x[0]) + open_w * (x[2] - x[0]) + open_n * (x[3] - x[0]) + open_s * (x[4] - x[0])

                we = -courant * jnp.minimum(fe, 0.0)
                ww = courant * jnp.maximum(fw, 0.0)
                wn = -courant * jnp.minimum(fn, 0.0)
                ws = courant * jnp.maximum(fs, 0.0)
                wc = 1.0 - courant * (
                    jnp.maximum(fe, 0.0) - jnp.minimum(fw, 0.0) + jnp.maximum(fn, 0.0) - jnp.minimum(fs, 0.0)
                )

                def carried(x):
                    return wc * x[0] + we * x[1] + ww * x[2] + wn * x[3] + ws * x[4]

                weights[cp, q, 0] = wc
                weights[cp, q, 1] = jnp.where(left, we, ww)
                weights[cp, q, 2] = jnp.where(left, ww, we)
                weights[cp, q, 3] = wn
                weights[cp, q, 4] = ws
                put(new, cp, q, (u[0] + time_step * (f * v[0] - slope_x) + viscosity * lap(u)) * w[0], 0)
                put(new, cp, q, (v[0] + time_step * (-f * u[0] - slope_y) + viscosity * lap(v)) * w[0], 1)
                warm = (carried(temp) + diffusion * lap(temp) + heating) * w[0]
                put(new, cp, q, warm, 2)
                put(new, cp, q, (carried(salt) + diffusion * lap(salt)) * w[0], 3)
                growth0[cp, q] = reaction * jnp.exp(warming * warm) * w[0]

    def carry(old, cp, q, t, weight):
        c, x, z, n, s = around(old, cp, q, t)
        return weight[0] * c + weight[1] * x + weight[2] * z + weight[3] * n + weight[4] * s

    def substep(old, new, first, last, finish):
        for cp in range(first, last):
            for q in range(nrt):
                p = carry(old, cp, q, 0, [weights[cp, q, k] for k in range(5)])
                flat[line(cp, q), :] = water_extinction + pigment_extinction * p
        span = pl.ds(first * nrt * ROWS8, (last - first) * nrt * ROWS8)
        extinct = flat[span, :]
        irradiance = jnp.exp(-(running_sums(extinct) - 0.5 * extinct))
        flat[span, :] = irradiance / (irradiance + light_half)
        for cp in range(first, last):
            for q in range(nrt):
                growth[cp, q] = flat[line(cp, q), :] * growth0[cp, q]

        blank = jnp.zeros((ROWS8, LANES), F32)

        def begin(cp, held):
            for q in range(nrt):
                weight = [weights[cp, q, k] for k in range(5)]
                parts = []
                for t in range(ntr):
                    a = carry(old, cp, q, t, weight)
                    new[cp, q + 1, t] = a
                    parts.append(a / (saturation + jnp.abs(a)))
                s = jnp.concatenate(parts + [blank], axis=0)
                high = s.astype(BF16)
                held[pl.ds(0, deep), pl.ds(q * LANES, LANES)] = high
                held[pl.ds(deep, deep), pl.ds(q * LANES, LANES)] = (s - high.astype(F32)).astype(BF16)

        def end(cp, held):
            for q in range(0, nrt, 2):
                group = range(q, min(q + 2, nrt))
                across = pl.ds(q * LANES, len(group) * LANES)
                high = held[pl.ds(0, deep), across]
                s = jnp.concatenate([high, held[pl.ds(deep, deep), across], high], axis=0)
                mixed = jnp.dot(mix_all, s, preferred_element_type=F32)
                for k, r in enumerate(group):
                    g = growth[cp, r]
                    for t in range(ntr):
                        block = mixed[t * ROWS8:(t + 1) * ROWS8, k * LANES:(k + 1) * LANES]
                        finish(cp, r, t, new[cp, r + 1, t] + g * block)

        begin(first, held_a)

        @pl.loop(0, (last - first) // 2 - 1)
        def _(k):
            cp = first + 2 * k
            begin(cp + 1, held_b)
            end(cp, held_a)
            begin(cp + 2, held_a)
            end(cp + 1, held_b)

        begin(last - 1, held_b)
        end(last - 2, held_a)
        end(last - 1, held_b)

    def finish_in(ref):
        def finish(cp, q, t, value):
            put(ref, cp, q, value, t)

        return finish

    def finish_out(cp, q, t, value):
        start = q * (ntr * inner) + t * inner + (cp - halo // 2)
        result[pl.ds(start, ROWS8, stride=nrt * ntr * inner), :] = value

    edge = halo // 2
    ocean_step(ocean_a, ocean_b, stock_a)
    substep(stock_a, stock_b, 0, ncp, finish_in(stock_b))
    substep(stock_b, stock_a, edge // 2, ncp - edge // 2, finish_in(stock_a))
    ocean_step(ocean_b, ocean_a, stock_a)
    substep(stock_a, stock_b, edge // 2, ncp - edge // 2, finish_in(stock_b))
    substep(stock_b, stock_a, edge, ncp - edge, finish_out)
    send = pltpu.make_async_copy(result.at[pl.ds(halo * ntr * inner, rows * ntr * inner)], out, sem.at[0])
    send.start()
    for f in range(4):
        for cp in range(inner):
            for q in range(nrt):
                sea[f, cp, pl.ds(q, ROWS8, stride=nrt), :] = ocean_a[cp + edge, q + 1, f]
            ocean_out[f, :, pl.ds(cp * LANES, LANES)] = sea[f, cp, pl.ds(halo, rows), :]
    send.wait()


def run_window(tile, south, north, west, ocean, east, interaction, ntr, ncp):
    rows = ocean.shape[1]
    halo = HALO
    nrt = (rows + 2 * halo) // ROWS8
    inner = ncp - halo
    anywhere = pl.BlockSpec(memory_space=pl.ANY)
    inside = pl.BlockSpec(memory_space=pltpu.VMEM)
    return pl.pallas_call(
        main_kernel,
        out_shape=(
            jax.ShapeDtypeStruct((4, rows, inner * LANES), F32),
            jax.ShapeDtypeStruct((rows * ntr * inner, LANES), F32),
        ),
        in_specs=[anywhere] * 3 + [inside] * 4,
        out_specs=(inside, anywhere),
        scratch_shapes=[
            pltpu.VMEM(((rows + 2 * halo) * (tile.shape[0] // rows), LANES), F32),
            pltpu.VMEM((ncp, nrt + 2, ntr, ROWS8, LANES), F32),
            pltpu.VMEM((ncp, nrt + 2, ntr, ROWS8, LANES), F32),
            pltpu.VMEM((4, ncp, rows + 2 * halo, LANES), F32),
            pltpu.VMEM((2, halo * 4 * ncp, LANES), F32),
            pltpu.VMEM((ncp, nrt + 2, 4, ROWS8, LANES), F32),
            pltpu.VMEM((ncp, nrt + 2, 4, ROWS8, LANES), F32),
            pltpu.VMEM((ncp, nrt + 2, ROWS8, LANES), F32),
            pltpu.VMEM((ncp, nrt + 2, ROWS8, LANES), F32),
            pltpu.VMEM((ncp, nrt, 5, ROWS8, LANES), F32),
            pltpu.VMEM((ncp, nrt, ROWS8, LANES), F32),
            pltpu.VMEM((ncp, nrt, ROWS8, LANES), F32),
            pltpu.VMEM((ncp * nrt * ROWS8, LANES), F32),
            pltpu.VMEM((2 * (ntr + 1) * ROWS8, nrt * LANES), BF16),
            pltpu.VMEM((2 * (ntr + 1) * ROWS8, nrt * LANES), BF16),
            pltpu.VMEM(((rows + 2 * halo) * ntr * inner, LANES), F32),
            pltpu.SemaphoreType.DMA((5,)),
        ],
        compiler_params=pltpu.CompilerParams(vmem_limit_bytes=40 * 2**20),
        name="window",
    )(tile, south, north, west, ocean, east, interaction)


def shift(array, axis, by):
    count = lax.axis_size(axis)
    if by > 0:
        return lax.ppermute(array, axis, [(i, i + 1) for i in range(count - 1)])
    return lax.ppermute(array, axis, [(i + 1, i) for i in range(count - 1)])


def shards(ocean_fields, tracers, wet_levels, interaction):
    tiles = lax.axis_size("gx")
    ntr = tracers.shape[0]
    rows = ocean_fields.shape[1]
    columns = wet_levels.shape[1]
    levels = tracers.shape[2] // columns
    lines = tracers.shape[2] // LANES
    pair = LANES // levels
    inner = lines // tiles
    edge = HALO // pair
    ncp = inner + 2 * edge

    margin = edge * LANES
    from_west = shift(ocean_fields[:, :, -margin:], "gx", 1)
    from_east = shift(ocean_fields[:, :, :margin], "gx", -1)
    depth = wet_levels.astype(F32).reshape(tiles, columns // tiles)
    blank = jnp.zeros((1, HALO), F32)
    depth = jnp.concatenate(
        [
            jnp.concatenate([blank, depth[:-1, -HALO:]], axis=0),
            depth,
            jnp.concatenate([depth[1:, :HALO], blank], axis=0),
            jnp.zeros((tiles, GROUP * LANES - columns // tiles - 2 * HALO), F32),
        ],
        axis=1,
    )
    sent = cut_windows(tracers.reshape(ntr, lines, 1, LANES), depth.reshape(tiles, GROUP, 1, LANES), tiles, ncp)
    tile = lax.all_to_all(sent.reshape(tiles, -1, LANES), "gx", split_axis=0, concat_axis=0, tiled=True)
    tile = tile.reshape(-1, LANES)
    to_north, to_south = row_messages(tile, from_west, ocean_fields, from_east, ncp)
    south = shift(to_north, "grp", 1)
    north = shift(to_south, "grp", -1)
    ocean_next, result = run_window(
        tile, south, north, from_west, ocean_fields, from_east, interaction, ntr, ncp
    )
    back = lax.all_to_all(result.reshape(tiles, ntr * inner, LANES), "gx", split_axis=0, concat_axis=0, tiled=True)
    back = back.reshape(tiles, ntr, inner, LANES).transpose(1, 0, 2, 3)
    return ocean_next, back.reshape(ntr, 1, lines * LANES)


def solution(mesh):
    placed = (P(None, "grp", "gx"), P(None, ("grp", "gx"), None), P(("grp", "gx"), None), P())
    return jax.shard_map(
        shards,
        mesh=mesh,
        in_specs=placed,
        out_specs=(P(None, "grp", "gx"), P(None, ("grp", "gx"), None)),
        check_vma=False,
    )
```

```python
import jax
import jax.numpy as jnp
from jax import lax
from jax.experimental import pallas as pl
from jax.experimental.pallas import tpu as pltpu
from jax.sharding import PartitionSpec as P

NC = 2
NB = 2
HALO = NC * NB

courant = 0.2
diffusion = 0.08
viscosity = 0.08
time_step = 0.1
thermal = 0.2
haline = 0.15
gravity = 0.1
coriolis = 0.5
coriolis_slope = 0.5
water_extinction = 0.04
pigment_extinction = 0.01
heating_rate = 0.5
light_half = 0.3
warming = 0.1
saturation = 0.5
reaction = 0.5

LANES = 128
ROWS8 = 8
F32 = jnp.float32
BF16 = jnp.bfloat16


GROUP = 4
PIECES = 4


def window_kernel(strip, wet_levels, out, big, depth, sem_in, sem_out):
    ntr, lines = strip.shape[0], strip.shape[1]
    tiles, groups = out.shape[0], (out.shape[1] - 1) // ntr
    step = lines // tiles
    edge = (big.shape[1] - lines) // 2
    span = lines // PIECES
    arrivals = [
        pltpu.make_async_copy(strip.at[:, pl.ds(p * span, span)], big.at[:, pl.ds(edge + p * span, span)], sem_in.at[p])
        for p in range(PIECES)
    ]
    for copy in arrivals:
        copy.start()
    zeros = jnp.zeros((ntr, edge, 1, LANES), F32)
    big[:, pl.ds(0, edge)] = zeros
    big[:, pl.ds(edge + lines, edge)] = zeros

    def sends(d):
        return [
            pltpu.make_async_copy(
                big.at[:, pl.ds(d * step + g * GROUP, GROUP)], out.at[d, pl.ds(g * ntr, ntr)], sem_out.at[d, g]
            )
            for g in range(groups)
        ]

    depth_out = pltpu.make_async_copy(depth, out.at[:, groups * ntr], sem_in.at[PIECES])

    first = 0
    for p in range(PIECES):
        arrivals[p].wait()
        last = tiles if p == PIECES - 1 else (span * (p + 1) + edge - groups * GROUP) // step + 1

        @pl.loop(first, last)
        def _(d):
            for copy in sends(d):
                copy.start()

        first = last

    columns = wet_levels.shape[1]
    depth[...] = jnp.zeros(depth.shape, F32)
    around = jnp.concatenate(
        [jnp.zeros((1, HALO), F32), wet_levels[...].astype(F32), jnp.zeros((1, LANES - HALO), F32)], axis=1
    )
    for d in range(tiles):
        depth[d, 0] = around[:, d * (columns // tiles):d * (columns // tiles) + LANES]
    depth_out.start()

    @pl.loop(0, tiles)
    def _(d):
        for copy in sends(d):
            copy.wait()

    depth_out.wait()


def cut_windows(strip, wet_levels, tiles, wide):
    ntr, lines = strip.shape[0], strip.shape[1]
    groups = wide // GROUP
    edge = (wide - lines // tiles) // 2
    anywhere = pl.BlockSpec(memory_space=pl.ANY)
    return pl.pallas_call(
        window_kernel,
        out_shape=jax.ShapeDtypeStruct((tiles, groups * ntr + 1, GROUP, 1, LANES), F32),
        in_specs=[anywhere, pl.BlockSpec(memory_space=pltpu.VMEM)],
        out_specs=anywhere,
        scratch_shapes=[
            pltpu.VMEM((ntr, lines + 2 * edge, 1, LANES), F32),
            pltpu.VMEM((tiles, GROUP, 1, LANES), F32),
            pltpu.SemaphoreType.DMA((PIECES + 1,)),
            pltpu.SemaphoreType.DMA((tiles, groups)),
        ],
        name="cut_windows",
    )(strip, wet_levels)


def edge_kernel(tile, west, ocean, east, to_north, to_south, lines, sem):
    rows = ocean.shape[1]
    halo = HALO
    wide = lines.shape[1] // halo
    per_row = tile.shape[0] // rows
    sides = ((to_north, rows - halo), (to_south, 0))
    copies = [
        pltpu.make_async_copy(
            tile.at[pl.ds(first * per_row, halo * per_row)], message.at[pl.ds(0, halo * per_row)], sem.at[k]
        )
        for k, (message, first) in enumerate(sides)
    ]
    for copy in copies:
        copy.start()
    for k, (message, first) in enumerate(sides):
        c = 0
        for f in range(4):
            for part in (west, ocean, east):
                for j in range(part.shape[2] // LANES):
                    lines[k, pl.ds(c, halo, stride=wide), :] = part[f, pl.ds(first, halo), pl.ds(j * LANES, LANES)]
                    c += 1
    more = [
        pltpu.make_async_copy(lines.at[k], message.at[pl.ds(halo * per_row, halo * wide)], sem.at[2 + k])
        for k, (message, first) in enumerate(sides)
    ]
    for copy in more:
        copy.start()
    for copy in copies + more:
        copy.wait()


def row_messages(tile, west, ocean, east, ncp):
    anywhere = pl.BlockSpec(memory_space=pl.ANY)
    inside = pl.BlockSpec(memory_space=pltpu.VMEM)
    message = jax.ShapeDtypeStruct((HALO * (tile.shape[0] // ocean.shape[1] + 4 * ncp), LANES), F32)
    return pl.pallas_call(
        edge_kernel,
        out_shape=(message, message),
        in_specs=[anywhere, inside, inside, inside],
        out_specs=(anywhere, anywhere),
        scratch_shapes=[
            pltpu.VMEM((2, HALO * 4 * ncp, LANES), F32),
            pltpu.SemaphoreType.DMA((4,)),
        ],
        compiler_params=pltpu.CompilerParams(vmem_limit_bytes=8 * 2**20),
        name="row_messages",
    )(tile, west, ocean, east)


def main_kernel(
    tile, south, north, west, ocean, east, mix_ref, ocean_out, out,
    raw, stock_a, stock_b, sea, beyond, ocean_a, ocean_b, press, wet, weights, growth0, growth, flat, held_a, held_b, result, sem,
):
    ncp, nrt, ntr = stock_a.shape[0], stock_a.shape[1] - 2, stock_a.shape[2]
    rows = ocean.shape[1]
    line_stride = tile.shape[0] // rows
    groups = ncp // GROUP
    halo = HALO
    inner = ncp - halo
    wide_ocean = 4 * ncp
    many = halo * line_stride
    copies = [
        pltpu.make_async_copy(tile, raw.at[pl.ds(many, rows * line_stride)], sem.at[0]),
        pltpu.make_async_copy(south.at[pl.ds(0, many)], raw.at[pl.ds(0, many)], sem.at[1]),
        pltpu.make_async_copy(north.at[pl.ds(0, many)], raw.at[pl.ds((halo + rows) * line_stride, many)], sem.at[2]),
        pltpu.make_async_copy(south.at[pl.ds(many, halo * wide_ocean)], beyond.at[0], sem.at[3]),
        pltpu.make_async_copy(north.at[pl.ds(many, halo * wide_ocean)], beyond.at[1], sem.at[4]),
    ]
    for copy in copies:
        copy.start()

    lane = lax.broadcasted_iota(jnp.int32, (ROWS8, LANES), 1)
    sub = lax.broadcasted_iota(jnp.int32, (ROWS8, LANES), 0)
    half = LANES // 2
    left = lane < half
    level_f = (lane % half).astype(F32)

    def swap(x):
        return pltpu.roll(x, half, 1)

    def put(ref, cp, q, value, *more):
        ref[(cp, q + 1, *more)] = value
        if q == 0:
            ref[(cp, nrt + 1, *more)] = pltpu.roll(value, ROWS8 - 1, 0)
        if q == nrt - 1:
            ref[(cp, 0, *more)] = pltpu.roll(value, 1, 0)

    def around(ref, cp, q, *more):
        right = ref[(jnp.minimum(cp + 1, ncp - 1), q + 1, *more)]
        leftward = ref[(jnp.maximum(cp - 1, 0), q + 1, *more)]
        centre = ref[(cp, q + 1, *more)]
        far = swap(jnp.where(left, right, leftward))
        return centre, swap(centre), far, ref[(cp, q + 2, *more)], ref[(cp, q, *more)]

    def five(ref, cp, q, *more):
        centre, swapped, far, cell_north, cell_south = around(ref, cp, q, *more)
        return centre, jnp.where(left, swapped, far), jnp.where(left, far, swapped), cell_north, cell_south

    row_id = lax.broadcasted_iota(jnp.int32, (LANES, LANES), 0)
    col_id = lax.broadcasted_iota(jnp.int32, (LANES, LANES), 1)
    upper = ((row_id <= col_id) & (row_id // half == col_id // half)).astype(F32).astype(BF16)

    def running_sums(x):
        high = x.astype(BF16)
        rest = x - high.astype(F32)
        middle = rest.astype(BF16)
        low = (rest - middle.astype(F32)).astype(BF16)
        return (
            jnp.dot(high, upper, preferred_element_type=F32)
            + jnp.dot(middle, upper, preferred_element_type=F32)
            + jnp.dot(low, upper, preferred_element_type=F32)
        )

    wide = ntr * ROWS8
    deep = (ntr + 1) * ROWS8
    pick = (lax.broadcasted_iota(jnp.int32, (wide, ntr), 0) // ROWS8 == lax.broadcasted_iota(jnp.int32, (wide, ntr), 1)).astype(F32).astype(BF16)
    pick_t = (lax.broadcasted_iota(jnp.int32, (ntr, deep), 1) // ROWS8 == lax.broadcasted_iota(jnp.int32, (ntr, deep), 0)).astype(F32).astype(BF16)
    same = lax.broadcasted_iota(jnp.int32, (wide, deep), 0) % ROWS8 == lax.broadcasted_iota(jnp.int32, (wide, deep), 1) % ROWS8

    def spread(part):
        tall = jnp.dot(pick, part, preferred_element_type=F32).astype(BF16)
        return jnp.where(same, jnp.dot(tall, pick_t, preferred_element_type=F32), 0.0)

    mix = mix_ref[...]
    mix_hi = mix.astype(BF16)
    mix_lo = (mix - mix_hi.astype(F32)).astype(BF16)
    spread_hi = spread(mix_hi)
    mix_all = jnp.concatenate([spread_hi, spread_hi, spread(mix_lo)], axis=1).astype(BF16)

    for copy in copies:
        copy.wait()

    for f in range(4):
        for cp in range(ncp):
            if cp < halo // 2:
                part, j = west, cp
            elif cp < ncp - halo // 2:
                part, j = ocean, cp - halo // 2
            else:
                part, j = east, cp - (ncp - halo // 2)
            sea[f, cp, pl.ds(0, halo), :] = beyond[0, pl.ds(f * ncp + cp, halo, stride=wide_ocean), :]
            sea[f, cp, pl.ds(halo, rows), :] = part[f, :, pl.ds(j * LANES, LANES)]
            sea[f, cp, pl.ds(halo + rows, halo), :] = beyond[1, pl.ds(f * ncp + cp, halo, stride=wide_ocean), :]
            for q in range(nrt):
                put(ocean_a, cp, q, sea[f, cp, pl.ds(q, ROWS8, stride=nrt), :], f)

    def spaced(start):
        return pl.ds(start, ROWS8, stride=nrt * line_stride)

    depths = jnp.concatenate(
        [raw[spaced(q * line_stride + groups * ntr * GROUP), :] for q in range(nrt)] + [jnp.zeros((ROWS8, LANES), F32)], axis=0
    ).astype(BF16)

    @pl.loop(0, ncp)
    def _(cp):
        of_pair = (row_id == 2 * cp + col_id // half).astype(F32).astype(BF16)
        depth = jnp.dot(depths, of_pair, preferred_element_type=F32)
        for q in range(nrt):
            base = q * line_stride + (cp // GROUP) * (ntr * GROUP) + cp % GROUP
            for t in range(ntr):
                put(stock_a, cp, q, raw[spaced(base + t * GROUP), :], t)
            put(wet, cp, q, (level_f < depth[q * ROWS8:(q + 1) * ROWS8]).astype(F32))

    first_row = lax.axis_index("grp") * rows - halo
    total_rows = rows * lax.axis_size("grp")

    def line(cp, q):
        return pl.ds((cp * nrt + q) * ROWS8, ROWS8)

    def ocean_step(old, new, stock, first, last):
        for cp in range(ncp):
            for q in range(nrt):
                flat[line(cp, q), :] = (haline * old[cp, q + 1, 3] - thermal * old[cp, q + 1, 2]) * wet[cp, q + 1]
        flat[...] = gravity * running_sums(flat[...])
        for cp in range(ncp):
            for q in range(nrt):
                put(press, cp, q, flat[line(cp, q), :])
        for cp in range(first, last):
            for q in range(nrt):
                flat[line(cp, q), :] = water_extinction + pigment_extinction * stock[cp, q + 1, 0]
        span = pl.ds(first * nrt * ROWS8, (last - first) * nrt * ROWS8)
        extinct_all = flat[span, :]
        flat[span, :] = heating_rate * extinct_all * jnp.exp(-(running_sums(extinct_all) - 0.5 * extinct_all))

        @pl.loop(first, last)
        def _(cp):
            for q in range(nrt):
                w = five(wet, cp, q)
                open_e, open_w, open_n, open_s = (w[0] * w[k] for k in range(1, 5))
                u = five(old, cp, q, 0)
                v = five(old, cp, q, 1)
                temp = five(old, cp, q, 2)
                salt = five(old, cp, q, 3)
                p = five(press, cp, q)
                fe = 0.5 * (u[0] + u[1]) * open_e
                fw = 0.5 * (u[0] + u[2]) * open_w
                fn = 0.5 * (v[0] + v[3]) * open_n
                fs = 0.5 * (v[0] + v[4]) * open_s
                slope_x = 0.5 * (open_e * (p[1] - p[0]) + open_w * (p[0] - p[2]))
                slope_y = 0.5 * (open_n * (p[3] - p[0]) + open_s * (p[0] - p[4]))
                row = (first_row + q + nrt * sub).astype(F32)
                f = coriolis + coriolis_slope * ((row + 0.5) / total_rows - 0.5)
                heating = flat[pl.ds(pl.multiple_of((cp * nrt + q) * ROWS8, ROWS8), ROWS8), :]

                def lap(x):
                    return open_e * (x[1] - x[0]) + open_w * (x[2] - x[0]) + open_n * (x[3] - x[0]) + open_s * (x[4] - x[0])

                we = -courant * jnp.minimum(fe, 0.0)
                ww = courant * jnp.maximum(fw, 0.0)
                wn = -courant * jnp.minimum(fn, 0.0)
                ws = courant * jnp.maximum(fs, 0.0)
                wc = 1.0 - courant * (
                    jnp.maximum(fe, 0.0) - jnp.minimum(fw, 0.0) + jnp.maximum(fn, 0.0) - jnp.minimum(fs, 0.0)
                )

                def carried(x):
                    return wc * x[0] + we * x[1] + ww * x[2] + wn * x[3] + ws * x[4]

                weights[cp, q, 0] = wc
                weights[cp, q, 1] = jnp.where(left, we, ww)
                weights[cp, q, 2] = jnp.where(left, ww, we)
                weights[cp, q, 3] = wn
                weights[cp, q, 4] = ws
                put(new, cp, q, (u[0] + time_step * (f * v[0] - slope_x) + viscosity * lap(u)) * w[0], 0)
                put(new, cp, q, (v[0] + time_step * (-f * u[0] - slope_y) + viscosity * lap(v)) * w[0], 1)
                warm = (carried(temp) + diffusion * lap(temp) + heating) * w[0]
                put(new, cp, q, warm, 2)
                put(new, cp, q, (carried(salt) + diffusion * lap(salt)) * w[0], 3)
                growth0[cp, q] = reaction * jnp.exp(warming * warm) * w[0]

    def carry(old, cp, q, t, weight):
        c, x, z, n, s = around(old, cp, q, t)
        return weight[0] * c + weight[1] * x + weight[2] * z + weight[3] * n + weight[4] * s

    def substep(old, new, first, last, finish):
        for cp in range(first, last):
            for q in range(nrt):
                p = carry(old, cp, q, 0, [weights[cp, q, k] for k in range(5)])
                flat[line(cp, q), :] = water_extinction + pigment_extinction * p
        span = pl.ds(first * nrt * ROWS8, (last - first) * nrt * ROWS8)
        extinct = flat[span, :]
        irradiance = jnp.exp(-(running_sums(extinct) - 0.5 * extinct))
        flat[span, :] = irradiance / (irradiance + light_half)
        for cp in range(first, last):
            for q in range(nrt):
                growth[cp, q] = flat[line(cp, q), :] * growth0[cp, q]

        blank = jnp.zeros((ROWS8, LANES), F32)

        def begin(cp, held):
            for q in range(nrt):
                weight = [weights[cp, q, k] for k in range(5)]
                parts = []
                for t in range(ntr):
                    a = carry(old, cp, q, t, weight)
                    new[cp, q + 1, t] = a
                    parts.append(a / (saturation + jnp.abs(a)))
                s = jnp.concatenate(parts + [blank], axis=0)
                high = s.astype(BF16)
                held[pl.ds(0, deep), pl.ds(q * LANES, LANES)] = high
                held[pl.ds(deep, deep), pl.ds(q * LANES, LANES)] = (s - high.astype(F32)).astype(BF16)

        def end(cp, held):
            for q in range(0, nrt, 2):
                group = range(q, min(q + 2, nrt))
                across = pl.ds(q * LANES, len(group) * LANES)
                high = held[pl.ds(0, deep), across]
                s = jnp.concatenate([high, held[pl.ds(deep, deep), across], high], axis=0)
                mixed = jnp.dot(mix_all, s, preferred_element_type=F32)
                for k, r in enumerate(group):
                    g = growth[cp, r]
                    for t in range(ntr):
                        block = mixed[t * ROWS8:(t + 1) * ROWS8, k * LANES:(k + 1) * LANES]
                        finish(cp, r, t, new[cp, r + 1, t] + g * block)

        begin(first, held_a)

        @pl.loop(0, (last - first) // 2 - 1)
        def _(k):
            cp = first + 2 * k
            begin(cp + 1, held_b)
            end(cp, held_a)
            begin(cp + 2, held_a)
            end(cp + 1, held_b)

        begin(last - 1, held_b)
        end(last - 2, held_a)
        end(last - 1, held_b)

    def finish_in(ref):
        def finish(cp, q, t, value):
            put(ref, cp, q, value, t)

        return finish

    def finish_out(cp, q, t, value):
        start = q * (ntr * inner) + t * inner + (cp - halo // 2)
        result[pl.ds(start, ROWS8, stride=nrt * ntr * inner), :] = value

    edge = halo // 2
    ocean_step(ocean_a, ocean_b, stock_a, 0, ncp)
    substep(stock_a, stock_b, 0, ncp, finish_in(stock_b))
    substep(stock_b, stock_a, edge // 2, ncp - edge // 2, finish_in(stock_a))
    ocean_step(ocean_b, ocean_a, stock_a, edge // 2, ncp - edge // 2)
    substep(stock_a, stock_b, edge // 2, ncp - edge // 2, finish_in(stock_b))
    substep(stock_b, stock_a, edge, ncp - edge, finish_out)
    send = pltpu.make_async_copy(result.at[pl.ds(halo * ntr * inner, rows * ntr * inner)], out, sem.at[0])
    send.start()
    for f in range(4):
        for cp in range(inner):
            for q in range(nrt):
                sea[f, cp, pl.ds(q, ROWS8, stride=nrt), :] = ocean_a[cp + edge, q + 1, f]
            ocean_out[f, :, pl.ds(cp * LANES, LANES)] = sea[f, cp, pl.ds(halo, rows), :]
    send.wait()


def run_window(tile, south, north, west, ocean, east, interaction, ntr, ncp):
    rows = ocean.shape[1]
    halo = HALO
    nrt = (rows + 2 * halo) // ROWS8
    inner = ncp - halo
    anywhere = pl.BlockSpec(memory_space=pl.ANY)
    inside = pl.BlockSpec(memory_space=pltpu.VMEM)
    return pl.pallas_call(
        main_kernel,
        out_shape=(
            jax.ShapeDtypeStruct((4, rows, inner * LANES), F32),
            jax.ShapeDtypeStruct((rows * ntr * inner, LANES), F32),
        ),
        in_specs=[anywhere] * 3 + [inside] * 4,
        out_specs=(inside, anywhere),
        scratch_shapes=[
            pltpu.VMEM(((rows + 2 * halo) * (tile.shape[0] // rows), LANES), F32),
            pltpu.VMEM((ncp, nrt + 2, ntr, ROWS8, LANES), F32),
            pltpu.VMEM((ncp, nrt + 2, ntr, ROWS8, LANES), F32),
            pltpu.VMEM((4, ncp, rows + 2 * halo, LANES), F32),
            pltpu.VMEM((2, halo * 4 * ncp, LANES), F32),
            pltpu.VMEM((ncp, nrt + 2, 4, ROWS8, LANES), F32),
            pltpu.VMEM((ncp, nrt + 2, 4, ROWS8, LANES), F32),
            pltpu.VMEM((ncp, nrt + 2, ROWS8, LANES), F32),
            pltpu.VMEM((ncp, nrt + 2, ROWS8, LANES), F32),
            pltpu.VMEM((ncp, nrt, 5, ROWS8, LANES), F32),
            pltpu.VMEM((ncp, nrt, ROWS8, LANES), F32),
            pltpu.VMEM((ncp, nrt, ROWS8, LANES), F32),
            pltpu.VMEM((ncp * nrt * ROWS8, LANES), F32),
            pltpu.VMEM((2 * (ntr + 1) * ROWS8, nrt * LANES), BF16),
            pltpu.VMEM((2 * (ntr + 1) * ROWS8, nrt * LANES), BF16),
            pltpu.VMEM(((rows + 2 * halo) * ntr * inner, LANES), F32),
            pltpu.SemaphoreType.DMA((5,)),
        ],
        compiler_params=pltpu.CompilerParams(vmem_limit_bytes=40 * 2**20),
        name="window",
    )(tile, south, north, west, ocean, east, interaction)


def shift(array, axis, by):
    count = lax.axis_size(axis)
    if by > 0:
        return lax.ppermute(array, axis, [(i, i + 1) for i in range(count - 1)])
    return lax.ppermute(array, axis, [(i + 1, i) for i in range(count - 1)])


def shards(ocean_fields, tracers, wet_levels, interaction):
    tiles = lax.axis_size("gx")
    ntr = tracers.shape[0]
    rows = ocean_fields.shape[1]
    columns = wet_levels.shape[1]
    levels = tracers.shape[2] // columns
    lines = tracers.shape[2] // LANES
    pair = LANES // levels
    inner = lines // tiles
    edge = HALO // pair
    ncp = inner + 2 * edge

    margin = edge * LANES
    from_west = shift(ocean_fields[:, :, -margin:], "gx", 1)
    from_east = shift(ocean_fields[:, :, :margin], "gx", -1)
    sent = cut_windows(tracers.reshape(ntr, lines, 1, LANES), wet_levels, tiles, ncp)
    tile = lax.all_to_all(sent.reshape(tiles, -1, LANES), "gx", split_axis=0, concat_axis=0, tiled=True)
    tile = tile.reshape(-1, LANES)
    to_north, to_south = row_messages(tile, from_west, ocean_fields, from_east, ncp)
    south = shift(to_north, "grp", 1)
    north = shift(to_south, "grp", -1)
    ocean_next, result = run_window(
        tile, south, north, from_west, ocean_fields, from_east, interaction, ntr, ncp
    )
    back = lax.all_to_all(result.reshape(tiles, ntr * inner, LANES), "gx", split_axis=0, concat_axis=0, tiled=True)
    back = back.reshape(tiles, ntr, inner, LANES).transpose(1, 0, 2, 3)
    return ocean_next, back.reshape(ntr, 1, lines * LANES)


def solution(mesh):
    placed = (P(None, "grp", "gx"), P(None, ("grp", "gx"), None), P(("grp", "gx"), None), P())
    return jax.shard_map(
        shards,
        mesh=mesh,
        in_specs=placed,
        out_specs=(P(None, "grp", "gx"), P(None, ("grp", "gx"), None)),
        check_vma=False,
    )
```
